32 devices in a mesh: grp: 2 (over y), tm: 8 (over z, x), apa: 2 (over core).
Axes of the slice: x: 2, y: 2, z: 4, core: 2. Of those that a mesh axis runs over, the one named last changes fastest.
Arguments:
- waveforms: bfloat16 [5120, 2048], P(('grp', 'apa'), 'tm'), parts along dimension 0, may hold values from -6 to 6
- time_kernel: bfloat16 [3, 64], replicated, may hold values from -0.75 to 0.75
- wire_slot: int32 [5120], P('grp'), parts along dimension 0, may hold values from 0 to 2559, each once
- tick_offset: int32 [5120], P('grp'), parts along dimension 0, may hold values from 0 to 63
- bad_channel: int32 [5120], P('grp'), parts along dimension 0, may hold values 0 or 1
- induction_real: float32 [2, 800], replicated, may hold values from 0.5 to 2
- induction_imaginary: float32 [2, 800], replicated, may hold values from -1 to 1
- induction_filter: float32 [2, 800], replicated, may hold values from 0.2 to 1
- collection_real: float32 [960], replicated, may hold values from 0.5 to 2
- collection_imaginary: float32 [960], replicated, may hold values from -1 to 1
- collection_filter: float32 [960], replicated, may hold values from 0.2 to 1
Outputs:
- deconvolved: float32 [5120, 2048], P('grp', ('tm', 'apa')), parts along dimension 0
The draws below stay inside these ranges and needn't reach their ends.
There are 2 independent parts, one for each index of `grp`. The reference program is written for one: setup_inputs(seed, part) draws one part's arguments, and reference() takes and returns one part's arrays. A program takes and returns all parts, laid end to end along the dimension named above; an argument that names none is the same for every part. Nothing has to cross between parts.
Inputs may be any that keep to these rules, and one draw needn't show every extreme that they name: A permutation: readout channel c is slot wire_slot[c] of the plane layout, whose assemblies hold 2560 slots each, U wires first, then V, then W. `bad_channel`: 1 marks a bad channel.
All inputs are finite; a program needn't handle non-finite values.
Results may differ from the reference program's by a relative error of at most 0.0051.
Values may be sent and summed in bfloat16 or wider, within the bound.
No kernel may reach another device: no remote copies, remote signals or barrier semaphores. Data moves between devices by JAX's collectives and lax.ppermute only.
A program may use at most 64 MiB of HBM per device.

```python
import math
import jax
import jax.numpy as jnp
from jax import lax

INDUCTION_WIRES = 800
COLLECTION_WIRES = 960
KERNEL_TAPS = 64
OFFSET_RANGE = 64
CHANNELS = 2560
TICKS = 2048


def touch_ends(values, key, low, high):
    dims = values.shape
    spot = [jax.random.randint(jax.random.fold_in(key, axis), (), 0, dims[axis]) for axis in range(len(dims))]
    values = values.at[tuple(spot)].set(low)
    longest = dims.index(max(dims))
    spot[longest] = (spot[longest] + 1) % dims[longest]
    return values.at[tuple(spot)].set(high)


def level_of(key, extent, pieces, low, high):
    factor_of, own = 1.0, jax.random.fold_in(key, 6)
    for position, shards_of in pieces:
        heights = jnp.exp(jax.random.uniform(jax.random.fold_in(own, position), (shards_of,), jnp.float32, low / len(pieces), high / len(pieces)))
        factor_of = factor_of * jnp.repeat(heights, extent[position] // shards_of).reshape([-1 if axis == position else 1 for axis in range(len(extent))])
    return factor_of


def centred(rng, shape, spread, most, shards=(), held_as=jnp.bfloat16):
    entries = jax.random.normal(rng, shape, jnp.float32) * spread
    if len(shards) > 0:
        entries = level_of(rng, shape, shards, -0.22, 0.18) * entries
    return jnp.clip(entries, min=-most, max=most).astype(held_as)


def setup_inputs(seed: int = 0, part: int = 0) -> dict:
    arg_keys = jax.random.split(jax.random.key(seed), 12)
    part_splits = jax.random.split(jax.random.fold_in(arg_keys[11], part), 12)
    waveforms = centred(part_splits[0], (CHANNELS, TICKS), 1.0, 6.0, ((0, 2), (1, 8)))
    time_kernel = centred(arg_keys[1], (3, KERNEL_TAPS), KERNEL_TAPS ** -0.5, 0.75)
    wire_slot = jax.random.permutation(part_splits[2], CHANNELS).astype(jnp.int32)
    tick_offset = touch_ends(jax.random.randint(part_splits[3], (CHANNELS,), 0, OFFSET_RANGE), jax.random.fold_in(part_splits[3], 1), 0, OFFSET_RANGE - 1).astype(jnp.int32)
    bad_channel = touch_ends((jax.random.randint(part_splits[4], (CHANNELS,), 0, 16) < 1).astype(jnp.int32), jax.random.fold_in(part_splits[4], 1), 0, 1)
    induction_real = jnp.clip(jax.random.uniform(arg_keys[5], (2, INDUCTION_WIRES), jnp.float32, 0.5, 2.0), 0.5, 2.0)
    induction_imaginary = jnp.clip(jax.random.uniform(arg_keys[6], (2, INDUCTION_WIRES), jnp.float32, -1.0, 1.0), -1.0, 1.0)
    induction_filter = jnp.clip(jnp.exp(jax.random.uniform(arg_keys[7], (2, INDUCTION_WIRES), jnp.float32, math.log(0.2), math.log(1.0))), 0.2, 1.0)
    collection_real = jnp.clip(jax.random.uniform(arg_keys[8], (COLLECTION_WIRES,), jnp.float32, 0.5, 2.0), 0.5, 2.0)
    collection_imaginary = jnp.clip(jax.random.uniform(arg_keys[9], (COLLECTION_WIRES,), jnp.float32, -1.0, 1.0), -1.0, 1.0)
    collection_filter = jnp.clip(jnp.exp(jax.random.uniform(arg_keys[10], (COLLECTION_WIRES,), jnp.float32, math.log(0.2), math.log(1.0))), 0.2, 1.0)
    return dict(waveforms=waveforms, time_kernel=time_kernel, wire_slot=wire_slot, tick_offset=tick_offset, bad_channel=bad_channel, induction_real=induction_real, induction_imaginary=induction_imaginary, induction_filter=induction_filter, collection_real=collection_real, collection_imaginary=collection_imaginary, collection_filter=collection_filter)


def slot_plane(slot_index):
    assembly_wires = 2 * INDUCTION_WIRES + COLLECTION_WIRES
    within = slot_index % assembly_wires
    return (within >= INDUCTION_WIRES).astype(jnp.int32) + (within >= 2 * INDUCTION_WIRES).astype(jnp.int32)


def fourier_tables(wire_count):
    positions = jnp.arange(wire_count, dtype=jnp.int32)
    phase_turns = (positions[:, None] * positions[None, :]) % wire_count
    phase_angle = phase_turns.astype(jnp.float32) * (2.0 * math.pi / wire_count)
    cosine = jnp.cos(phase_angle).astype(jnp.bfloat16)
    sine_table = jnp.sin(phase_angle).astype(jnp.bfloat16)
    forward = jnp.concatenate([cosine, sine_table], 0)
    backward = jnp.concatenate([cosine, -sine_table], 1)
    return forward, backward


def wire_deconvolve(plane_rows, tables, response_real, response_imaginary, filter_gain):
    forward, backward = tables
    wire_count = plane_rows.shape[0]
    magnitude = response_real * response_real + response_imaginary * response_imaginary
    ratio_real = (filter_gain * response_real / magnitude)[:, None]
    ratio_imaginary = (-filter_gain * response_imaginary / magnitude)[:, None]
    signal = lax.optimization_barrier(plane_rows).astype(jnp.float32)
    spectrum = jnp.dot(forward.astype(jnp.float32), signal, preferred_element_type=jnp.float32, precision=lax.Precision.HIGHEST)
    cosine_part = spectrum[:wire_count]
    sine_part = spectrum[wire_count:]
    product = jnp.concatenate([cosine_part * ratio_real + sine_part * ratio_imaginary, cosine_part * ratio_imaginary - sine_part * ratio_real], 0)
    product = lax.optimization_barrier(product.astype(jnp.bfloat16)).astype(jnp.float32)
    result = jnp.dot(backward.astype(jnp.float32), product, preferred_element_type=jnp.float32, precision=lax.Precision.HIGHEST)
    return result * (1.0 / wire_count)


def deconvolve_planes(ordered, induction_real, induction_imaginary, induction_filter, collection_real, collection_imaginary, collection_filter):
    assembly_wires = 2 * INDUCTION_WIRES + COLLECTION_WIRES
    induction_tables = fourier_tables(INDUCTION_WIRES)
    collection_tables = fourier_tables(COLLECTION_WIRES)
    results = []
    for assembly in range(ordered.shape[0] // assembly_wires):
        first_row = assembly * assembly_wires
        for plane_index in range(2):
            row_start = first_row + plane_index * INDUCTION_WIRES
            results.append(wire_deconvolve(ordered[row_start:row_start + INDUCTION_WIRES], induction_tables, induction_real[plane_index], induction_imaginary[plane_index], induction_filter[plane_index]))
        row_start = first_row + 2 * INDUCTION_WIRES
        results.append(wire_deconvolve(ordered[row_start:row_start + COLLECTION_WIRES], collection_tables, collection_real, collection_imaginary, collection_filter))
    return jnp.concatenate(results, 0)


def time_filter(waveforms, time_kernel, wire_slot, tick_offset, bad_channel):
    tick_count = waveforms.shape[1]
    channel_count = waveforms.shape[0]
    kernel_spectrum = jnp.fft.rfft(time_kernel.astype(jnp.float32), n=tick_count, axis=1)
    frequency = jnp.arange(tick_count // 2 + 1, dtype=jnp.int32)
    block_rows = math.gcd(channel_count, 128)
    block_count = channel_count // block_rows
    plane_ids = slot_plane(wire_slot)
    keep_factor = (1 - bad_channel).astype(jnp.float32)

    def filter_block(inputs):
        signal, planes_here, offsets, kept_rows = inputs
        spectrum = jnp.fft.rfft(signal.astype(jnp.float32) * kept_rows[:, None], axis=1)
        phase_turns = (frequency[None, :] * offsets[:, None]) % tick_count
        phase_angle = phase_turns.astype(jnp.float32) * (2.0 * math.pi / tick_count)
        rotated = spectrum * jnp.exp(-1j * phase_angle) * kernel_spectrum[planes_here]
        return jnp.fft.irfft(rotated, n=tick_count, axis=1).astype(jnp.bfloat16)

    inputs = (waveforms.reshape(block_count, block_rows, tick_count), plane_ids.reshape(block_count, block_rows), tick_offset.reshape(block_count, block_rows), keep_factor.reshape(block_count, block_rows))
    return lax.map(filter_block, inputs).reshape(channel_count, tick_count)


def reference(waveforms, time_kernel, wire_slot, tick_offset, bad_channel, induction_real, induction_imaginary, induction_filter, collection_real, collection_imaginary, collection_filter):
    filtered = time_filter(waveforms, time_kernel, wire_slot, tick_offset, bad_channel)
    channel_count = wire_slot.shape[0]
    inverse = jnp.zeros((channel_count,), jnp.int32).at[wire_slot].set(jnp.arange(channel_count, dtype=jnp.int32))
    ordered = filtered[inverse]
    return deconvolve_planes(ordered, induction_real, induction_imaginary, induction_filter, collection_real, collection_imaginary, collection_filter)
```

```python
import functools
import math

import jax
import jax.numpy as jnp
import numpy as np
from jax import lax
from jax.experimental import pallas as pl
from jax.experimental.pallas import tpu as pltpu
from jax.sharding import PartitionSpec as P

OFFSET_RANGE = 64
LANES = 128
VMEM = pltpu.VMEM
SMEM = pltpu.SMEM


def padded(count):
    return -(-count // LANES) * LANES


def wire_base(wires):
    return padded(wires)


def wire_tables(wires):
    base = wire_base(wires)
    spans = 2 * base // LANES
    m = np.arange(wires, dtype=np.int64)
    coarse = (np.arange(spans, dtype=np.int64)[:, None] * LANES - base) * m[None, :] % wires
    fine = m[:, None] * np.arange(LANES, dtype=np.int64)[None, :] % wires
    turn = 2.0 * math.pi / wires
    return (
        np.cos(coarse * turn).astype(np.float32),
        np.sin(coarse * turn).astype(np.float32),
        np.cos(fine * turn).astype(np.float32),
        np.sin(fine * turn).astype(np.float32),
    )


def lane_roll(row, rows):
    r = lax.broadcasted_iota(jnp.int32, (rows, LANES), 0)
    l = lax.broadcasted_iota(jnp.int32, (rows, LANES), 1)
    spread = jnp.broadcast_to(row, (rows, LANES))
    return jnp.take_along_axis(spread, (l - r) & (LANES - 1), axis=1, mode="promise_in_bounds")


def response_kernel(wires_by_plane, re0, im0, fl0, re1, im1, fl1, *refs):
    tables = [refs[0:4], refs[4:8]]
    outs = refs[8:11]
    r = lax.broadcasted_iota(jnp.int32, (LANES, LANES), 0)
    l = lax.broadcasted_iota(jnp.int32, (LANES, LANES), 1)
    for plane, wires in enumerate(wires_by_plane):
        ca, sa, cb, sb = tables[0 if plane < 2 else 1]
        if plane < 2:
            real, imag, gain = (ref[plane : plane + 1, :] for ref in (re0, im0, fl0))
        else:
            real, imag, gain = (ref[...] for ref in (re1, im1, fl1))
        scale = gain / (real * real + imag * imag) * (1.0 / wires)
        ratio_re = real * scale
        ratio_im = -imag * scale
        u = ca[...] * ratio_re + sa[...] * ratio_im
        v = ca[...] * ratio_im - sa[...] * ratio_re
        dot = functools.partial(
            jnp.dot, precision=lax.Precision.HIGHEST, preferred_element_type=jnp.float32
        )
        taps = dot(u, cb[...]) + dot(v, sb[...])
        out = outs[plane]
        previous = lane_roll(taps[0:1, :], LANES)
        for span in range(taps.shape[0]):
            here = lane_roll(taps[span : span + 1, :], LANES)
            out[:, span * LANES : (span + 1) * LANES] = jnp.where(l >= r, here, previous).astype(
                jnp.bfloat16
            )
            previous = here


def rotated(block, offsets):
    l = lax.broadcasted_iota(jnp.int32, block.shape, 1)
    return jnp.take_along_axis(
        block.astype(jnp.float32), (l - offsets) & (LANES - 1), axis=1, mode="promise_in_bounds"
    )


def by_plane(sums, planes):
    zero = jnp.zeros_like(planes, dtype=jnp.float32)
    picked = jnp.where(planes == 2, sums[:, 2 * LANES :], zero)
    picked = jnp.where(planes == 1, sums[:, LANES : 2 * LANES], picked)
    return jnp.where(planes == 0, sums[:, :LANES], picked)


def own_kernel(step, wave, code, taps, high_out, low_out, table_out):
    r = lax.broadcasted_iota(jnp.int32, (LANES, LANES), 0)
    l = lax.broadcasted_iota(jnp.int32, (LANES, LANES), 1)
    for plane in range(3):
        rolled = lane_roll(taps[plane : plane + 1, :], LANES)
        cols = slice(plane * LANES, (plane + 1) * LANES)
        table_out[:LANES, cols] = jnp.where(l < r, rolled, 0.0).astype(jnp.bfloat16)
        table_out[LANES:, cols] = jnp.where(l >= r, rolled, 0.0).astype(jnp.bfloat16)

    def body(i, carry):
        rows = pl.ds(pl.multiple_of(i * step, step), step)
        word = code[rows, :]
        offsets = word & (OFFSET_RANGE - 1)
        planes = word // OFFSET_RANGE
        lane = lax.broadcasted_iota(jnp.int32, word.shape, 1)
        early = rotated(wave[rows, :LANES], offsets)
        late = rotated(wave[rows, LANES:], offsets)
        wrapped = lane < offsets
        low = jnp.where(wrapped, 0.0, early).astype(jnp.bfloat16)
        both = jnp.concatenate([early, jnp.where(wrapped, early, late)], 1).astype(jnp.bfloat16)
        table = table_out[...]
        low_sum = jnp.dot(low, table[LANES:, :], preferred_element_type=jnp.float32)
        high_sum = jnp.dot(both, table, preferred_element_type=jnp.float32)
        low_out[rows, :] = by_plane(low_sum, planes)
        high_out[rows, :] = by_plane(high_sum, planes).astype(jnp.bfloat16)
        return carry

    lax.fori_loop(0, wave.shape[0] // step, body, 0)


def halo_kernel(step, side, halo, code, table_ref, low_main, high, own_out, other_out):
    def body(i, carry):
        rows = pl.ds(pl.multiple_of(i * step, step), step)
        word = code[rows, :]
        offsets = word & (OFFSET_RANGE - 1)
        planes = word // OFFSET_RANGE
        lane = lax.broadcasted_iota(jnp.int32, word.shape, 1)
        early = rotated(halo[rows, :], offsets)
        both = jnp.concatenate([early, jnp.where(lane < offsets, early, 0.0)], 1).astype(
            jnp.bfloat16
        )
        sums = jnp.dot(both, table_ref[...], preferred_element_type=jnp.float32)
        low = low_main[rows, :] + by_plane(sums, planes)
        upper = high[rows, :].astype(jnp.float32)
        first = side[0] == 0
        own_out[rows, :] = jnp.where(first, low, upper).astype(jnp.bfloat16)
        other_out[rows, :] = jnp.where(first, upper, low).astype(jnp.bfloat16)
        return carry

    lax.fori_loop(0, halo.shape[0] // step, body, 0)


def place_rows(source, slots, first_row, target, unroll):
    count = source.shape[0]

    def body(i, carry):
        start = i * unroll
        for k in range(unroll):
            slot = slots[first_row + start + k]
            target[pl.ds(slot, 1), :] = source[pl.ds(start + k, 1), :]
        return carry

    lax.fori_loop(0, count // unroll, body, 0)


def place_kernel(gaps, side, slots, own, ordered, wide):
    wide[...] = own[...].astype(jnp.float32)
    for start, stop in gaps:
        ordered[start:stop, :] = jnp.zeros((stop - start, LANES), jnp.float32)
    place_rows(wide, slots, side[0] * own.shape[0], ordered, 16)


def final_kernel(layout, side, slots, other, half_placed, resp0, resp1, resp2, out, ordered, wide):
    count = other.shape[0]
    wide[...] = other[...].astype(jnp.float32)
    ordered[...] = half_placed[...]
    place_rows(wide, slots, (1 - side[0]) * count, ordered, 16)
    for (start, wires, row), resp in zip(layout, (resp0, resp1, resp2)):
        depth = padded(wires)
        base = wire_base(wires)
        data = ordered[start : start + depth, :].astype(jnp.bfloat16)
        for block in range(depth // LANES):
            valid = min(LANES, wires - block * LANES)
            left = base - block * LANES
            result = jnp.dot(
                resp[:, left : left + depth], data, preferred_element_type=jnp.float32
            )
            out[row + block * LANES : row + block * LANES + valid, :] = result[:valid, :]


def local(
    waveforms,
    time_kernel,
    wire_slot,
    tick_offset,
    bad_channel,
    induction_real,
    induction_imaginary,
    induction_filter,
    collection_real,
    collection_imaginary,
    collection_filter,
):
    induction = induction_real.shape[1]
    collection = collection_real.shape[0]
    wires_by_plane = (induction, induction, collection)
    taps = time_kernel.shape[1]
    rows, ticks = waveforms.shape
    channels = wire_slot.shape[0]
    assert ticks == 2 * LANES and taps + OFFSET_RANGE == LANES
    assert channels == 2 * rows and channels == 2 * induction + collection

    ring = lax.axis_size("tm")
    halo = lax.ppermute(
        waveforms[:, ticks - LANES :], "tm", [(i, (i + 1) % ring) for i in range(ring)]
    )

    side = lax.axis_index("apa")
    side_word = side.reshape(1).astype(jnp.int32)
    plane = (wire_slot >= induction).astype(jnp.int32) + (wire_slot >= 2 * induction).astype(
        jnp.int32
    )
    code = tick_offset + OFFSET_RANGE * jnp.where(bad_channel == 0, plane, 3)
    code = lax.dynamic_slice_in_dim(code, side * rows, rows)
    code = jnp.broadcast_to(code[:, None], (rows, LANES))
    gap = padded(induction) - induction
    spread_slot = wire_slot + gap * plane
    padded_taps = jnp.pad(time_kernel.astype(jnp.float32), ((0, 0), (0, LANES - taps)))

    bases = [wire_base(w) for w in wires_by_plane]
    vm = pl.BlockSpec(memory_space=VMEM)
    sm = pl.BlockSpec(memory_space=SMEM)

    tables = [jnp.asarray(t) for w in (induction, collection) for t in wire_tables(w)]
    responses = pl.pallas_call(
        functools.partial(response_kernel, wires_by_plane),
        out_shape=[jax.ShapeDtypeStruct((LANES, 2 * b), jnp.bfloat16) for b in bases],
        in_specs=[vm] * 14,
        out_specs=[vm] * 3,
        cost_estimate=pl.CostEstimate(flops=2 * 10**8, bytes_accessed=4 * 10**6, transcendentals=0),
        name="response",
    )(
        induction_real,
        induction_imaginary,
        induction_filter,
        collection_real[None],
        collection_imaginary[None],
        collection_filter[None],
        *tables,
    )

    step = 256
    high, low_main, table = pl.pallas_call(
        functools.partial(own_kernel, step),
        out_shape=[
            jax.ShapeDtypeStruct((rows, LANES), jnp.bfloat16),
            jax.ShapeDtypeStruct((rows, LANES), jnp.float32),
            jax.ShapeDtypeStruct((2 * LANES, 3 * LANES), jnp.bfloat16),
        ],
        in_specs=[vm] * 3,
        out_specs=[vm] * 3,
        cost_estimate=pl.CostEstimate(flops=10**9, bytes_accessed=3 * 10**6, transcendentals=0),
        name="own_window",
    )(waveforms, code, padded_taps)

    own, other = pl.pallas_call(
        functools.partial(halo_kernel, step),
        out_shape=[jax.ShapeDtypeStruct((rows, LANES), jnp.bfloat16)] * 2,
        in_specs=[sm] + [vm] * 5,
        out_specs=[vm] * 2,
        name="halo_window",
    )(side_word, halo, code, table, low_main, high)

    received = lax.ppermute(other, "apa", [(0, 1), (1, 0)])

    layout = []
    start = row = 0
    gaps = []
    for wires in wires_by_plane:
        layout.append((start, wires, row))
        gaps.append((start + wires, start + padded(wires)))
        start += padded(wires)
        row += wires

    half_placed = pl.pallas_call(
        functools.partial(place_kernel, gaps),
        out_shape=jax.ShapeDtypeStruct((start, LANES), jnp.float32),
        in_specs=[sm, sm, vm],
        out_specs=vm,
        scratch_shapes=[pltpu.VMEM((rows, LANES), jnp.float32)],
        cost_estimate=pl.CostEstimate(flops=10**6, bytes_accessed=3 * 10**6, transcendentals=0),
        name="place_own",
    )(side_word, spread_slot, own)

    return pl.pallas_call(
        functools.partial(final_kernel, layout),
        out_shape=jax.ShapeDtypeStruct((channels, LANES), jnp.float32),
        in_specs=[sm, sm] + [vm] * 5,
        out_specs=vm,
        scratch_shapes=[
            pltpu.VMEM((start, LANES), jnp.float32),
            pltpu.VMEM((rows, LANES), jnp.float32),
        ],
        name="place_and_mix",
    )(side_word, spread_slot, received, half_placed, *responses)


def solution(mesh):
    placed = (P(("grp", "apa"), "tm"), P(), P("grp"), P("grp"), P("grp")) + (P(),) * 6
    return jax.shard_map(
        local, mesh=mesh, in_specs=placed, out_specs=P("grp", ("tm", "apa")), check_vma=False
    )
```

```python
import functools
import math

import jax
import jax.numpy as jnp
import numpy as np
from jax import lax
from jax.experimental import pallas as pl
from jax.experimental.pallas import tpu as pltpu
from jax.sharding import PartitionSpec as P

OFFSET_RANGE = 64
LANES = 128
VMEM = pltpu.VMEM
SMEM = pltpu.SMEM
KERNEL_VMEM = 16 * 2**20
STEP = 256
UNROLL = 32
COARSE_ROWS = 16


def padded(count):
    return -(-count // LANES) * LANES


def wire_tables(wires_by_plane):
    widest = max(wires_by_plane)
    coarse_rows, fine_rows = [], []
    for wires in wires_by_plane[1:]:
        base = padded(wires)
        m = np.arange(wires, dtype=np.int64)
        step = np.arange(2 * base // LANES, dtype=np.int64)[:, None] * LANES - base
        turn = 2.0 * math.pi / wires
        coarse = step * m[None, :] % wires * turn
        fine = m[:, None] * np.arange(LANES, dtype=np.int64)[None, :] % wires * turn
        for table in (np.cos(coarse), np.sin(coarse)):
            full = np.zeros((COARSE_ROWS, widest), np.float32)
            full[: table.shape[0], :wires] = table
            coarse_rows.append(full)
        fine_rows.append(np.concatenate([np.cos(fine), np.sin(fine)], 1).astype(np.float32))
    return np.concatenate(coarse_rows, 0), np.concatenate(fine_rows, 0)


def lane_roll(row, rows):
    r = lax.broadcasted_iota(jnp.int32, (rows, LANES), 0)
    l = lax.broadcasted_iota(jnp.int32, (rows, LANES), 1)
    spread = jnp.broadcast_to(row, (rows, LANES))
    return jnp.take_along_axis(spread, (l - r) & (LANES - 1), axis=1, mode="promise_in_bounds")


def make_responses(wires_by_plane, induction, collection, coarse, fine, outs):
    r = lax.broadcasted_iota(jnp.int32, (LANES, LANES), 0)
    l = lax.broadcasted_iota(jnp.int32, (LANES, LANES), 1)
    dot = functools.partial(
        jnp.dot, precision=lax.Precision.HIGHEST, preferred_element_type=jnp.float32
    )
    for plane, wires in enumerate(wires_by_plane):
        first = 0 if plane < 2 else 2 * COARSE_ROWS
        ca = coarse[first : first + COARSE_ROWS, :wires]
        sa = coarse[first + COARSE_ROWS : first + 2 * COARSE_ROWS, :wires]
        first = 0 if plane < 2 else wires_by_plane[0]
        cb = fine[first : first + wires, :LANES]
        sb = fine[first : first + wires, LANES:]
        if plane < 2:
            real, imag, gain = (ref[plane : plane + 1, :] for ref in induction)
        else:
            real, imag, gain = (ref[...] for ref in collection)
        scale = gain / (real * real + imag * imag) * (1.0 / wires)
        ratio_re = real * scale
        ratio_im = -imag * scale
        u = ca * ratio_re + sa * ratio_im
        v = ca * ratio_im - sa * ratio_re
        taps = dot(u, cb) + dot(v, sb)
        out = outs[plane]
        previous = lane_roll(taps[0:1, :], LANES)
        for span in range(out.shape[1] // LANES):
            here = lane_roll(taps[span : span + 1, :], LANES)
            out[:, span * LANES : (span + 1) * LANES] = jnp.where(l >= r, here, previous).astype(
                jnp.bfloat16
            )
            previous = here


def rotated(block, offsets):
    l = lax.broadcasted_iota(jnp.int32, block.shape, 1)
    return jnp.take_along_axis(
        block.astype(jnp.float32), (l - offsets) & (LANES - 1), axis=1, mode="promise_in_bounds"
    )


def by_plane(sums, planes):
    zero = jnp.zeros_like(planes, dtype=jnp.float32)
    picked = jnp.where(planes == 2, sums[:, 2 * LANES :], zero)
    picked = jnp.where(planes == 1, sums[:, LANES : 2 * LANES], picked)
    return jnp.where(planes == 0, sums[:, :LANES], picked)


def cut_kernel(wave, tail, sem):
    copy = pltpu.make_async_copy(wave.at[:, LANES:], tail, sem)
    copy.start()
    copy.wait()


def window_kernel(wires_by_plane, step, side, *refs):
    count = 13
    sources, refs = refs[:count], refs[count:]
    high_out, low_out, table_out, code_out = refs[:4]
    responses = refs[4:7]
    held, refs = refs[7 : 7 + count], refs[7 + count :]
    words, wide_taps, sems = refs
    copies = [
        pltpu.make_async_copy(source, target, sems.at[i])
        for i, (source, target) in enumerate(zip(sources, held))
    ]
    for copy in copies:
        copy.start()
    slots, offset_rows, bad_rows, kernel_taps, wave = held[:5]
    induction, collection = held[5:8], held[8:11]
    coarse, fine = held[11:13]
    for copy in copies[:5]:
        copy.wait()
    r = lax.broadcasted_iota(jnp.int32, (LANES, LANES), 0)
    l = lax.broadcasted_iota(jnp.int32, (LANES, LANES), 1)

    wide_taps[...] = jnp.zeros_like(wide_taps)
    wide_taps[0:3, 0 : kernel_taps.shape[1]] = kernel_taps[...].astype(jnp.float32)
    for plane in range(3):
        rolled = lane_roll(wide_taps[plane : plane + 1, :], LANES)
        cols = slice(plane * LANES, (plane + 1) * LANES)
        table_out[:LANES, cols] = jnp.where(l < r, rolled, 0.0).astype(jnp.bfloat16)
        table_out[LANES:, cols] = jnp.where(l >= r, rolled, 0.0).astype(jnp.bfloat16)

    slot = slots[...]
    one, two = wires_by_plane[0], wires_by_plane[0] + wires_by_plane[1]
    planes = (slot >= one).astype(jnp.int32) + (slot >= two).astype(jnp.int32)
    planes = jnp.where(bad_rows[...] == 0, planes, 3)
    words[...] = offset_rows[...] + OFFSET_RANGE * planes

    groups = wave.shape[0] // LANES
    first_group = side[0] * groups

    def spread(i, carry):
        row = jnp.broadcast_to(words[pl.ds(first_group + i, 1), :], (LANES, LANES))
        code_out[pl.ds(pl.multiple_of(i * LANES, LANES), LANES), :] = row.T
        return carry

    lax.fori_loop(0, groups, spread, 0)

    def body(i, carry):
        rows = pl.ds(pl.multiple_of(i * step, step), step)
        word = code_out[rows, :]
        offsets = word & (OFFSET_RANGE - 1)
        plane = word // OFFSET_RANGE
        lane = lax.broadcasted_iota(jnp.int32, word.shape, 1)
        early = rotated(wave[rows, :LANES], offsets)
        late = rotated(wave[rows, LANES:], offsets)
        wrapped = lane < offsets
        low = jnp.where(wrapped, 0.0, early).astype(jnp.bfloat16)
        both = jnp.concatenate([early, jnp.where(wrapped, early, late)], 1).astype(jnp.bfloat16)
        table = table_out[...]
        low_sum = jnp.dot(low, table[LANES:, :], preferred_element_type=jnp.float32)
        high_sum = jnp.dot(both, table, preferred_element_type=jnp.float32)
        low_out[rows, :] = by_plane(low_sum, plane)
        high_out[rows, :] = by_plane(high_sum, plane).astype(jnp.bfloat16)
        return carry

    lax.fori_loop(0, wave.shape[0] // step, body, 0)
    for copy in copies[5:]:
        copy.wait()
    make_responses(wires_by_plane, induction, collection, coarse, fine, responses)


def halo_kernel(step, side, halo, code, table_ref, low_main, high, own_out, other_out):
    def body(i, carry):
        rows = pl.ds(pl.multiple_of(i * step, step), step)
        word = code[rows, :]
        offsets = word & (OFFSET_RANGE - 1)
        planes = word // OFFSET_RANGE
        lane = lax.broadcasted_iota(jnp.int32, word.shape, 1)
        early = rotated(halo[rows, :], offsets)
        both = jnp.concatenate([early, jnp.where(lane < offsets, early, 0.0)], 1).astype(
            jnp.bfloat16
        )
        sums = jnp.dot(both, table_ref[...], preferred_element_type=jnp.float32)
        low = low_main[rows, :] + by_plane(sums, planes)
        upper = high[rows, :].astype(jnp.float32)
        first = side[0] == 0
        own_out[rows, :] = jnp.where(first, low, upper).astype(jnp.bfloat16)
        other_out[rows, :] = jnp.where(first, upper, low).astype(jnp.bfloat16)
        return carry

    lax.fori_loop(0, halo.shape[0] // step, body, 0)


def place_rows(source, slots, first_row, target, unroll):
    count = source.shape[0]

    def body(i, carry):
        start = pl.multiple_of(i * unroll, unroll)
        near = slots.at[pl.ds(first_row + start, unroll)]
        for k in range(unroll):
            target[pl.ds(near[k], 1), :] = source[pl.ds(start + k, 1), :]
        return carry

    lax.fori_loop(0, count // unroll, body, 0)


def place_kernel(side, slots, own, ordered, wide):
    wide[...] = own[...].astype(jnp.float32)
    place_rows(wide, slots, side[0] * own.shape[0], ordered, UNROLL)


def final_kernel(layout, side, slots, other, half_placed, *refs):
    responses, out, wide, ordered, mixed, sems = refs[:3], *refs[3:]
    count = other.shape[0]
    wide[...] = other[...].astype(jnp.float32)
    ordered[...] = half_placed[...]
    place_rows(wide, slots, (1 - side[0]) * count, ordered, UNROLL)
    copies = []
    for plane, ((start, wires), resp) in enumerate(zip(layout, responses)):
        base = padded(wires)
        data = ordered[start : start + wires, :].astype(jnp.bfloat16)
        for block in range(base // LANES):
            valid = min(LANES, wires - block * LANES)
            left = base - block * LANES
            result = jnp.dot(
                resp[:, left : left + wires], data, preferred_element_type=jnp.float32
            )
            top = start + block * LANES
            mixed[top : top + valid, :] = result[:valid, :]
        span = pl.ds(start, wires)
        copies.append(pltpu.make_async_copy(mixed.at[span], out.at[span], sems.at[plane]))
        copies[-1].start()
    for copy in copies:
        copy.wait()


def local(
    waveforms,
    time_kernel,
    wire_slot,
    tick_offset,
    bad_channel,
    induction_real,
    induction_imaginary,
    induction_filter,
    collection_real,
    collection_imaginary,
    collection_filter,
):
    induction = induction_real.shape[1]
    collection = collection_real.shape[0]
    wires_by_plane = (induction, induction, collection)
    taps = time_kernel.shape[1]
    rows, ticks = waveforms.shape
    channels = wire_slot.shape[0]
    assert ticks == 2 * LANES and taps + OFFSET_RANGE == LANES
    assert channels == 2 * rows and channels == 2 * induction + collection

    ring = lax.axis_size("tm")
    hbm = pl.BlockSpec(memory_space=pltpu.HBM)
    keep = functools.partial(pltpu.with_memory_space_constraint, memory_space=pltpu.HBM)
    params = pltpu.CompilerParams(vmem_limit_bytes=KERNEL_VMEM)
    tail = pl.pallas_call(
        cut_kernel,
        out_shape=jax.ShapeDtypeStruct((rows, LANES), jnp.bfloat16),
        in_specs=[hbm],
        out_specs=pl.BlockSpec(memory_space=VMEM),
        scratch_shapes=[pltpu.SemaphoreType.DMA],
        compiler_params=params,
        name="cut_tail",
    )(keep(waveforms))
    halo = lax.ppermute(tail, "tm", [(i, (i + 1) % ring) for i in range(ring)])

    side = lax.axis_index("apa")
    side_word = side.reshape(1).astype(jnp.int32)
    vm = pl.BlockSpec(memory_space=VMEM)
    sm = pl.BlockSpec(memory_space=SMEM)
    shape = jax.ShapeDtypeStruct

    def by_lanes(vector):
        return vector.reshape(channels // LANES, LANES)

    inputs = [
        by_lanes(wire_slot),
        by_lanes(tick_offset),
        by_lanes(bad_channel),
        time_kernel,
        waveforms,
        induction_real,
        induction_imaginary,
        induction_filter,
        collection_real[None],
        collection_imaginary[None],
        collection_filter[None],
        *(jnp.asarray(t) for t in wire_tables(wires_by_plane)),
    ]
    window = pl.pallas_call(
        functools.partial(window_kernel, wires_by_plane, STEP),
        out_shape=[
            shape((rows, LANES), jnp.bfloat16),
            shape((rows, LANES), jnp.float32),
            shape((2 * LANES, 3 * LANES), jnp.bfloat16),
            shape((rows, LANES), jnp.int32),
        ]
        + [shape((LANES, 2 * padded(w)), jnp.bfloat16) for w in wires_by_plane],
        in_specs=[sm] + [hbm] * len(inputs),
        out_specs=[vm] * 7,
        scratch_shapes=[pltpu.VMEM(x.shape, x.dtype) for x in inputs]
        + [
            pltpu.VMEM((channels // LANES, LANES), jnp.int32),
            pltpu.VMEM((8, LANES), jnp.float32),
            pltpu.SemaphoreType.DMA((len(inputs),)),
        ],
        compiler_params=params,
        cost_estimate=pl.CostEstimate(flops=10**9, bytes_accessed=8 * 10**6, transcendentals=0),
        name="own_window",
    )(side_word, *map(keep, inputs))
    high, low_main, table, code = window[:4]
    responses = window[4:]

    own, other = pl.pallas_call(
        functools.partial(halo_kernel, STEP),
        out_shape=[shape((rows, LANES), jnp.bfloat16)] * 2,
        in_specs=[sm] + [vm] * 5,
        out_specs=[vm] * 2,
        compiler_params=params,
        cost_estimate=pl.CostEstimate(flops=10**8, bytes_accessed=2 * 10**6, transcendentals=0),
        name="halo_window",
    )(side_word, halo, code, table, low_main, high)

    received = lax.ppermute(other, "apa", [(0, 1), (1, 0)])

    half_placed = pl.pallas_call(
        place_kernel,
        out_shape=shape((channels, LANES), jnp.float32),
        in_specs=[sm, sm, vm],
        out_specs=vm,
        scratch_shapes=[pltpu.VMEM((rows, LANES), jnp.float32)],
        compiler_params=params,
        cost_estimate=pl.CostEstimate(flops=10**6, bytes_accessed=3 * 10**6, transcendentals=0),
        name="place_own",
    )(side_word, wire_slot, own)

    layout = []
    start = 0
    for wires in wires_by_plane:
        layout.append((start, wires))
        start += wires
    return pl.pallas_call(
        functools.partial(final_kernel, layout),
        out_shape=shape((channels, LANES), jnp.float32),
        in_specs=[sm, sm] + [vm] * 5,
        out_specs=pl.BlockSpec(memory_space=pl.ANY),
        scratch_shapes=[
            pltpu.VMEM((rows, LANES), jnp.float32),
            pltpu.VMEM((channels, LANES), jnp.float32),
            pltpu.VMEM((channels, LANES), jnp.float32),
            pltpu.SemaphoreType.DMA((3,)),
        ],
        compiler_params=params,
        name="place_and_mix",
    )(side_word, wire_slot, received, half_placed, *responses)


def solution(mesh):
    placed = (P(("grp", "apa"), "tm"), P(), P("grp"), P("grp"), P("grp")) + (P(),) * 6
    return jax.shard_map(
        local, mesh=mesh, in_specs=placed, out_specs=P("grp", ("tm", "apa")), check_vma=False
    )
```

```python
import functools
import math

import jax
import jax.numpy as jnp
import numpy as np
from jax import lax
from jax.experimental import pallas as pl
from jax.experimental.pallas import tpu as pltpu
from jax.sharding import PartitionSpec as P


OFFSET_RANGE = 64
LANES = 128
VMEM = pltpu.VMEM
SMEM = pltpu.SMEM
KERNEL_VMEM = 16 * 2**20
STEP = 320
LAST_ROWS = 640


def padded(count):
    return -(-count // LANES) * LANES


def wire_tables(wires_by_plane):
    widest = max(wires_by_plane)
    coarse_rows, fine_rows = [], []
    for wires in wires_by_plane[1:]:
        base = padded(wires // 2)
        m = np.arange(wires, dtype=np.int64)
        step = np.arange(2 * base // LANES, dtype=np.int64)[:, None] * LANES - base
        turn = 2.0 * math.pi / wires
        coarse = step * m[None, :] % wires * turn
        fine = m[:, None] * np.arange(LANES, dtype=np.int64)[None, :] % wires * turn
        for table in (np.cos(coarse), np.sin(coarse)):
            full = np.zeros((2, step.shape[0], widest), np.float32)
            full[0, :, :wires:2] = table[:, ::2]
            full[1, :, 1:wires:2] = table[:, 1::2]
            coarse_rows.append(full.reshape(-1, widest))
        fine_rows.append(np.concatenate([np.cos(fine), np.sin(fine)], 1).astype(np.float32))
    fine = np.concatenate(fine_rows, 0)
    high = fine.astype(jnp.bfloat16)
    low = (fine - high.astype(np.float32)).astype(jnp.bfloat16)
    return np.concatenate(coarse_rows, 0), np.concatenate([high, low], 1)


def lane_roll(row, rows):
    r = lax.broadcasted_iota(jnp.int32, (rows, LANES), 0)
    l = lax.broadcasted_iota(jnp.int32, (rows, LANES), 1)
    spread = jnp.broadcast_to(row, (rows, LANES))
    return jnp.take_along_axis(spread, (l - r) & (LANES - 1), axis=1, mode="promise_in_bounds")


def split_dot(left, high, low):
    upper = left.astype(jnp.bfloat16)
    lower = (left - upper.astype(jnp.float32)).astype(jnp.bfloat16)
    rows = left.shape[0]
    both = jnp.dot(
        jnp.concatenate([upper, lower], 0), high, preferred_element_type=jnp.float32
    )
    return both[:rows] + both[rows:] + jnp.dot(upper, low, preferred_element_type=jnp.float32)


def make_responses(wires_by_plane, induction, collection, coarse, fine, outs):
    r = lax.broadcasted_iota(jnp.int32, (LANES, LANES), 0)
    l = lax.broadcasted_iota(jnp.int32, (LANES, LANES), 1)
    for plane, wires in enumerate(wires_by_plane):
        out = outs[plane]
        spans = out.shape[1] // LANES
        first = 0 if plane < 2 else coarse.shape[0] - 4 * spans
        ca = coarse[first : first + 2 * spans, :wires]
        sa = coarse[first + 2 * spans : first + 4 * spans, :wires]
        first = 0 if plane < 2 else wires_by_plane[0]
        rows = slice(first, first + wires)
        if plane < 2:
            real, imag, gain = (ref[plane : plane + 1, :] for ref in induction)
        else:
            real, imag, gain = (ref[...] for ref in collection)
        scale = gain / (real * real + imag * imag) * (1.0 / wires)
        ratio_re = real * scale
        ratio_im = -imag * scale
        u = ca * ratio_re + sa * ratio_im
        v = ca * ratio_im - sa * ratio_re
        taps = split_dot(u, fine[rows, :LANES], fine[rows, 2 * LANES : 3 * LANES])
        taps = taps + split_dot(v, fine[rows, LANES : 2 * LANES], fine[rows, 3 * LANES :])
        for parity in range(2):
            top = slice(parity * LANES, (parity + 1) * LANES)
            previous = None
            for span in range(spans):
                row = parity * spans + span
                here = lane_roll(taps[row : row + 1, :], LANES)
                before = here if previous is None else previous
                out[top, span * LANES : (span + 1) * LANES] = jnp.where(l >= r, here, before).astype(
                    jnp.bfloat16
                )
                previous = here


def rotated(block, offsets):
    l = lax.broadcasted_iota(jnp.int32, block.shape, 1)
    return jnp.take_along_axis(
        block.astype(jnp.float32), (l - offsets) & (LANES - 1), axis=1, mode="promise_in_bounds"
    )


def by_plane(sums, planes):
    zero = jnp.zeros_like(planes, dtype=jnp.float32)
    picked = jnp.where(planes == 2, sums[:, 2 * LANES :], zero)
    picked = jnp.where(planes == 1, sums[:, LANES : 2 * LANES], picked)
    return jnp.where(planes == 0, sums[:, :LANES], picked)


def cut_kernel(wave, *refs):
    tails, sem = refs[:-1], refs[-1]
    first = 0
    copies = []
    for i, tail in enumerate(tails):
        rows = pl.ds(first, tail.shape[0])
        copies.append(pltpu.make_async_copy(wave.at[rows, LANES:], tail, sem.at[i]))
        copies[-1].start()
        first += tail.shape[0]
    for copy in copies:
        copy.wait()


def window_kernel(wires_by_plane, step, side, *refs):
    count = 13
    sources, refs = refs[:count], refs[count:]
    high_out, low_out, table_out, code_out, near_out, far_out = refs[:6]
    responses = refs[6:9]
    held, refs = refs[9 : 9 + count], refs[9 + count :]
    words, wide_taps, sems = refs
    copies = [
        pltpu.make_async_copy(source, target, sems.at[i])
        for i, (source, target) in enumerate(zip(sources, held))
    ]
    for copy in copies:
        copy.start()
    slots, offset_rows, bad_rows, kernel_taps, wave = held[:5]
    induction, collection = held[5:8], held[8:11]
    coarse, fine = held[11:13]
    for copy in copies[:5]:
        copy.wait()
    r = lax.broadcasted_iota(jnp.int32, (LANES, LANES), 0)
    l = lax.broadcasted_iota(jnp.int32, (LANES, LANES), 1)

    wide_taps[...] = jnp.zeros_like(wide_taps)
    wide_taps[0:3, 0 : kernel_taps.shape[1]] = kernel_taps[...].astype(jnp.float32)
    for plane in range(3):
        rolled = lane_roll(wide_taps[plane : plane + 1, :], LANES)
        cols = slice(plane * LANES, (plane + 1) * LANES)
        table_out[:LANES, cols] = jnp.where(l < r, rolled, 0.0).astype(jnp.bfloat16)
        table_out[LANES:, cols] = jnp.where(l >= r, rolled, 0.0).astype(jnp.bfloat16)

    slot = slots[...]
    one, two = wires_by_plane[0], wires_by_plane[0] + wires_by_plane[1]
    planes = (slot >= one).astype(jnp.int32) + (slot >= two).astype(jnp.int32)
    planes = jnp.where(bad_rows[...] == 0, planes, 3)
    words[...] = offset_rows[...] + OFFSET_RANGE * planes

    groups = wave.shape[0] // LANES
    first_group = side[0] * groups

    near_out[0:groups, :] = slots[pl.ds(first_group, groups), :]
    far_out[0:groups, :] = slots[pl.ds((1 - side[0]) * groups, groups), :]

    def spread(i, carry):
        row = jnp.broadcast_to(words[pl.ds(first_group + i, 1), :], (LANES, LANES))
        code_out[pl.ds(pl.multiple_of(i * LANES, LANES), LANES), :] = row.T
        return carry

    lax.fori_loop(0, groups, spread, 0)

    def body(i, carry):
        rows = pl.ds(pl.multiple_of(i * step, step), step)
        word = code_out[rows, :]
        offsets = word & (OFFSET_RANGE - 1)
        plane = word // OFFSET_RANGE
        lane = lax.broadcasted_iota(jnp.int32, word.shape, 1)
        early = rotated(wave[rows, :LANES], offsets)
        late = rotated(wave[rows, LANES:], offsets)
        wrapped = lane < offsets
        low = jnp.where(wrapped, 0.0, early).astype(jnp.bfloat16)
        both = jnp.concatenate([early, jnp.where(wrapped, early, late)], 1).astype(jnp.bfloat16)
        table = table_out[...]
        low_sum = jnp.dot(low, table[LANES:, :], preferred_element_type=jnp.float32)
        high_sum = jnp.dot(both, table, preferred_element_type=jnp.float32)
        low_out[rows, :] = by_plane(low_sum, plane)
        high_out[rows, :] = by_plane(high_sum, plane).astype(jnp.bfloat16)
        return carry

    lax.fori_loop(0, wave.shape[0] // step, body, 0)
    for copy in copies[5:]:
        copy.wait()
    make_responses(wires_by_plane, induction, collection, coarse, fine, responses)


def halo_kernel(step, first, side, halo, code, table_ref, low_main, high, own_out, other_out):
    def body(i, carry):
        here = pl.ds(pl.multiple_of(i * step, step), step)
        rows = pl.ds(pl.multiple_of(first + i * step, step), step)
        word = code[rows, :]
        offsets = word & (OFFSET_RANGE - 1)
        planes = word // OFFSET_RANGE
        lane = lax.broadcasted_iota(jnp.int32, word.shape, 1)
        early = rotated(halo[here, :], offsets)
        both = jnp.concatenate([early, jnp.where(lane < offsets, early, 0.0)], 1).astype(
            jnp.bfloat16
        )
        sums = jnp.dot(both, table_ref[...], preferred_element_type=jnp.float32)
        low = low_main[rows, :] + by_plane(sums, planes)
        upper = high[rows, :].astype(jnp.float32)
        inner = side[0] == 0
        own_out[here, :] = jnp.where(inner, low, upper).astype(jnp.bfloat16)
        other_out[here, :] = jnp.where(inner, upper, low).astype(jnp.bfloat16)
        return carry

    lax.fori_loop(0, halo.shape[0] // step, body, 0)


def place_rows(source, wide, slots, first, target):
    count = source.shape[0]
    wide[0:count, :] = source[...].astype(jnp.float32)
    for k in range(count):
        slot = slots[(first + k) // LANES, (first + k) % LANES]
        target[pl.ds(slot, 1), :] = wide[k : k + 1, :]


def start_kernel(near, own, placed, wide):
    place_rows(own, wide, near, 0, placed)


def middle_kernel(near, far, own, other, before, placed, wide):
    del before
    place_rows(own, wide, near, other.shape[0], placed)
    place_rows(other, wide, far, 0, placed)


def final_kernel(layout, first, far, other, before, *refs):
    responses, out, ordered, wide, mixed, sems = refs[:3], *refs[3:]
    del before
    place_rows(other, wide, far, first, ordered)
    copies = []
    for plane, ((start, wires), resp) in enumerate(zip(layout, responses)):
        half = wires // 2
        base = padded(half)
        front = ordered[start : start + half, :]
        back = ordered[start + half : start + wires, :]
        total = (front + back).astype(jnp.bfloat16)
        change = (front - back).astype(jnp.bfloat16)
        for block in range(base // LANES):
            valid = min(LANES, half - block * LANES)
            columns = slice(base - block * LANES, base - block * LANES + half)
            even = jnp.dot(resp[:valid, columns], total, preferred_element_type=jnp.float32)
            odd = jnp.dot(
                resp[LANES : LANES + valid, columns], change, preferred_element_type=jnp.float32
            )
            top = start + block * LANES
            mixed[top : top + valid, :] = even + odd
            mixed[top + half : top + half + valid, :] = even - odd
        for part in range(2):
            span = pl.ds(start + part * half, half)
            copies.append(
                pltpu.make_async_copy(mixed.at[span], out.at[span], sems.at[2 * plane + part])
            )
            copies[-1].start()
    for copy in copies:
        copy.wait()


def deconvolve(
    waveforms,
    time_kernel,
    wire_slot,
    tick_offset,
    bad_channel,
    induction_real,
    induction_imaginary,
    induction_filter,
    collection_real,
    collection_imaginary,
    collection_filter,
):
    induction = induction_real.shape[1]
    collection = collection_real.shape[0]
    wires_by_plane = (induction, induction, collection)
    taps = time_kernel.shape[1]
    rows, ticks = waveforms.shape
    channels = wire_slot.shape[0]
    assert ticks == 2 * LANES and taps + OFFSET_RANGE == LANES
    assert channels == 2 * rows and channels == 2 * induction + collection

    ring = lax.axis_size("tm")
    hbm = pl.BlockSpec(memory_space=pltpu.HBM)
    keep = functools.partial(pltpu.with_memory_space_constraint, memory_space=pltpu.HBM)
    params = pltpu.CompilerParams(vmem_limit_bytes=KERNEL_VMEM)
    parts = (rows - LAST_ROWS, LAST_ROWS)
    tails = pl.pallas_call(
        cut_kernel,
        out_shape=[jax.ShapeDtypeStruct((part, LANES), jnp.bfloat16) for part in parts],
        in_specs=[hbm],
        out_specs=[pl.BlockSpec(memory_space=VMEM)] * 2,
        scratch_shapes=[pltpu.SemaphoreType.DMA((2,))],
        compiler_params=params,
        name="cut_tail",
    )(keep(waveforms))
    onward = [(i, (i + 1) % ring) for i in range(ring)]
    first_halo = lax.ppermute(tails[0], "tm", onward)
    last_halo = lax.ppermute(tails[1], "tm", onward)

    side = lax.axis_index("apa")
    side_word = side.reshape(1).astype(jnp.int32)
    vm = pl.BlockSpec(memory_space=VMEM)
    sm = pl.BlockSpec(memory_space=SMEM)
    shape = jax.ShapeDtypeStruct

    def by_lanes(vector):
        return vector.reshape(channels // LANES, LANES)

    inputs = [
        by_lanes(wire_slot),
        by_lanes(tick_offset),
        by_lanes(bad_channel),
        time_kernel,
        waveforms,
        induction_real,
        induction_imaginary,
        induction_filter,
        collection_real[None],
        collection_imaginary[None],
        collection_filter[None],
        *(jnp.asarray(t) for t in wire_tables(wires_by_plane)),
    ]
    window = pl.pallas_call(
        functools.partial(window_kernel, wires_by_plane, 256),
        out_shape=[
            shape((rows, LANES), jnp.bfloat16),
            shape((rows, LANES), jnp.float32),
            shape((2 * LANES, 3 * LANES), jnp.bfloat16),
            shape((rows, LANES), jnp.int32),
            shape((rows // LANES, LANES), jnp.int32),
            shape((rows // LANES, LANES), jnp.int32),
        ]
        + [shape((2 * LANES, 2 * padded(w // 2)), jnp.bfloat16) for w in wires_by_plane],
        in_specs=[sm] + [hbm] * len(inputs),
        out_specs=[vm] * 9,
        scratch_shapes=[pltpu.VMEM(x.shape, x.dtype) for x in inputs]
        + [
            pltpu.VMEM((channels // LANES, LANES), jnp.int32),
            pltpu.VMEM((8, LANES), jnp.float32),
            pltpu.SemaphoreType.DMA((len(inputs),)),
        ],
        compiler_params=params,
        cost_estimate=pl.CostEstimate(flops=10**9, bytes_accessed=8 * 10**6, transcendentals=0),
        name="own_window",
    )(side_word, *map(keep, inputs))
    high, low_main, table, code, near, far = window[:6]
    responses = window[6:]

    def finish(halo, first):
        count = halo.shape[0]
        return pl.pallas_call(
            functools.partial(halo_kernel, STEP, first),
            out_shape=[shape((count, LANES), jnp.bfloat16)] * 2,
            in_specs=[sm] + [vm] * 5,
            out_specs=[vm] * 2,
            compiler_params=params,
            cost_estimate=pl.CostEstimate(
                flops=10**5 * count, bytes_accessed=10**3 * count, transcendentals=0
            ),
            name="halo_window",
        )(side_word, halo, code, table, low_main, high)

    def place(kernel, aliases, *operands):
        return pl.pallas_call(
            kernel,
            out_shape=shape((channels, LANES), jnp.float32),
            in_specs=[sm if x.dtype == jnp.int32 else vm for x in operands],
            out_specs=vm,
            scratch_shapes=[pltpu.VMEM((rows, LANES), jnp.float32)],
            input_output_aliases=aliases,
            compiler_params=params,
            cost_estimate=pl.CostEstimate(flops=10**6, bytes_accessed=10**6, transcendentals=0),
        )(*operands)

    partner = [(0, 1), (1, 0)]
    own_first, other_first = finish(first_halo, 0)
    received_first = lax.ppermute(other_first, "apa", partner)
    placed = place(start_kernel, {}, near, own_first)
    own_last, other_last = finish(last_halo, parts[0])
    received_last = lax.ppermute(other_last, "apa", partner)
    placed = place(middle_kernel, {4: 0}, near, far, own_last, received_first, placed)

    layout = []
    start = 0
    for wires in wires_by_plane:
        layout.append((start, wires))
        start += wires
    return pl.pallas_call(
        functools.partial(final_kernel, layout, parts[0]),
        out_shape=[shape((channels, LANES), jnp.float32)] * 2,
        in_specs=[sm] + [vm] * 5,
        out_specs=[pl.BlockSpec(memory_space=pl.ANY), vm],
        scratch_shapes=[
            pltpu.VMEM((rows, LANES), jnp.float32),
            pltpu.VMEM((channels, LANES), jnp.float32),
            pltpu.SemaphoreType.DMA((6,)),
        ],
        input_output_aliases={2: 1},
        compiler_params=params,
        name="place_and_mix",
    )(far, received_last, placed, *responses)[0]


def solution(mesh):
    placed = (P(("grp", "apa"), "tm"), P(), P("grp"), P("grp"), P("grp")) + (P(),) * 6
    return jax.shard_map(
        deconvolve, mesh=mesh, in_specs=placed, out_specs=P("grp", ("tm", "apa")), check_vma=False
    )
```

```python
import functools
import math

import jax
import jax.numpy as jnp
import numpy as np
from jax import lax
from jax.experimental import pallas as pl
from jax.experimental.pallas import tpu as pltpu
from jax.sharding import PartitionSpec as P


OFFSET_RANGE = 64
LANES = 128
VMEM = pltpu.VMEM
SMEM = pltpu.SMEM
KERNEL_VMEM = 16 * 2**20
STEP = 256
LAST_ROWS = 512


def padded(count):
    return -(-count // LANES) * LANES


def wire_tables(wires_by_plane):
    widest = max(wires_by_plane)
    coarse_rows, fine_rows = [], []
    for wires in wires_by_plane[1:]:
        base = padded(wires // 2)
        m = np.arange(wires, dtype=np.int64)
        step = np.arange(2 * base // LANES, dtype=np.int64)[:, None] * LANES - base
        turn = 2.0 * math.pi / wires
        coarse = step * m[None, :] % wires * turn
        fine = m[:, None] * np.arange(LANES, dtype=np.int64)[None, :] % wires * turn
        for table in (np.cos(coarse), np.sin(coarse)):
            full = np.zeros((2, step.shape[0], widest), np.float32)
            full[0, :, :wires:2] = table[:, ::2]
            full[1, :, 1:wires:2] = table[:, 1::2]
            coarse_rows.append(full.reshape(-1, widest))
        fine_rows.append(np.concatenate([np.cos(fine), np.sin(fine)], 1).astype(np.float32))
    fine = np.concatenate(fine_rows, 0)
    high = fine.astype(jnp.bfloat16)
    low = (fine - high.astype(np.float32)).astype(jnp.bfloat16)
    return np.concatenate(coarse_rows, 0), np.concatenate([high, low], 1)


def take_lanes(rows, lanes):
    return lax.gather(
        rows,
        lanes[..., None],
        lax.GatherDimensionNumbers(
            offset_dims=(),
            collapsed_slice_dims=(1,),
            start_index_map=(1,),
            operand_batching_dims=(0,),
            start_indices_batching_dims=(0,),
        ),
        slice_sizes=(1, 1),
        mode=lax.GatherScatterMode.PROMISE_IN_BOUNDS,
    )


def lane_roll(row, rows):
    r = lax.broadcasted_iota(jnp.int32, (rows, LANES), 0)
    l = lax.broadcasted_iota(jnp.int32, (rows, LANES), 1)
    return take_lanes(jnp.broadcast_to(row, (rows, LANES)), (l - r) & (LANES - 1))


def split_dot(left, high, low):
    upper = left.astype(jnp.bfloat16)
    lower = (left - upper.astype(jnp.float32)).astype(jnp.bfloat16)
    rows = left.shape[0]
    both = jnp.dot(
        jnp.concatenate([upper, lower], 0), high, preferred_element_type=jnp.float32
    )
    return both[:rows] + both[rows:] + jnp.dot(upper, low, preferred_element_type=jnp.float32)


def make_responses(wires_by_plane, induction, collection, coarse, fine, outs):
    r = lax.broadcasted_iota(jnp.int32, (LANES, LANES), 0)
    l = lax.broadcasted_iota(jnp.int32, (LANES, LANES), 1)
    for plane, wires in enumerate(wires_by_plane):
        out = outs[plane]
        spans = out.shape[1] // LANES
        first = 0 if plane < 2 else coarse.shape[0] - 4 * spans
        ca = coarse[first : first + 2 * spans, :wires]
        sa = coarse[first + 2 * spans : first + 4 * spans, :wires]
        first = 0 if plane < 2 else wires_by_plane[0]
        rows = slice(first, first + wires)
        if plane < 2:
            real, imag, gain = (ref[plane : plane + 1, :] for ref in induction)
        else:
            real, imag, gain = (ref[...] for ref in collection)
        scale = gain / (real * real + imag * imag) * (1.0 / wires)
        ratio_re = real * scale
        ratio_im = -imag * scale
        u = ca * ratio_re + sa * ratio_im
        v = ca * ratio_im - sa * ratio_re
        taps = split_dot(u, fine[rows, :LANES], fine[rows, 2 * LANES : 3 * LANES])
        taps = taps + split_dot(v, fine[rows, LANES : 2 * LANES], fine[rows, 3 * LANES :])
        for parity in range(2):
            top = slice(parity * LANES, (parity + 1) * LANES)
            previous = None
            for span in range(spans):
                row = parity * spans + span
                here = lane_roll(taps[row : row + 1, :], LANES)
                before = here if previous is None else previous
                out[top, span * LANES : (span + 1) * LANES] = jnp.where(l >= r, here, before).astype(
                    jnp.bfloat16
                )
                previous = here


def delays(word):
    lane = lax.broadcasted_iota(jnp.int32, word.shape, 1)
    source = (lane - word) & (LANES - 1)
    return source, source > lane


def by_plane(sums, word):
    picked = jnp.where(word < 3 * LANES, sums[:, 2 * LANES :], 0.0)
    picked = jnp.where(word < 2 * LANES, sums[:, LANES : 2 * LANES], picked)
    return jnp.where(word < LANES, sums[:, :LANES], picked)


def start_all(pairs, sems):
    copies = [
        pltpu.make_async_copy(source, target, sems.at[i])
        for i, (source, target) in enumerate(pairs)
    ]
    for copy in copies:
        copy.start()
    return copies


def cut_kernel(wave, *refs):
    tails, sems = refs[:-1], refs[-1]
    pairs = []
    first = 0
    for tail in tails:
        pairs.append((wave.at[pl.ds(first, tail.shape[0]), LANES:], tail))
        first += tail.shape[0]
    for copy in start_all(pairs, sems):
        copy.wait()


def response_kernel(wires_by_plane, *refs):
    make_responses(wires_by_plane, refs[0:3], refs[3:6], refs[6], refs[7], refs[8:11])


def fill_table(kernel_taps, wide_taps, table_out):
    r = lax.broadcasted_iota(jnp.int32, (LANES, LANES), 0)
    l = lax.broadcasted_iota(jnp.int32, (LANES, LANES), 1)
    wide_taps[...] = jnp.zeros_like(wide_taps)
    wide_taps[0:3, 0 : kernel_taps.shape[1]] = kernel_taps[...].astype(jnp.float32)
    for plane in range(3):
        rolled = lane_roll(wide_taps[plane : plane + 1, :], LANES)
        cols = slice(plane * LANES, (plane + 1) * LANES)
        table_out[:LANES, cols] = jnp.where(l < r, rolled, 0.0).astype(jnp.bfloat16)
        table_out[LANES:, cols] = jnp.where(l >= r, rolled, 0.0).astype(jnp.bfloat16)


def filter_window(wires_by_plane, side, front, tails, small, table, outs, words):
    high_out, low_out, code_out = outs
    slots, offset_rows, bad_rows = small
    one, two = wires_by_plane[0], wires_by_plane[0] + wires_by_plane[1]
    slot = slots[...]
    planes = (slot >= one).astype(jnp.int32) + (slot >= two).astype(jnp.int32)
    planes = jnp.where(bad_rows[...] == 0, planes, 3)
    words[...] = offset_rows[...] + LANES * planes
    groups = front.shape[0] // LANES
    for i in range(groups):
        row = jnp.broadcast_to(words[pl.ds(side[0] * groups + i, 1), :], (LANES, LANES))
        code_out[i * LANES : (i + 1) * LANES, :] = row.T

    first = 0
    for tail in tails:
        step = math.gcd(tail.shape[0], STEP)
        for top in range(0, tail.shape[0], step):
            rows = slice(first + top, first + top + step)
            word = code_out[rows, :]
            source, wrapped = delays(word)
            early = take_lanes(front[rows, :].astype(jnp.float32), source)
            late = take_lanes(tail[top : top + step, :].astype(jnp.float32), source)
            low = jnp.where(wrapped, 0.0, early).astype(jnp.bfloat16)
            both = jnp.concatenate([early, jnp.where(wrapped, early, late)], 1)
            low_sum = jnp.dot(low, table[LANES:, :], preferred_element_type=jnp.float32)
            high_sum = jnp.dot(
                both.astype(jnp.bfloat16), table[...], preferred_element_type=jnp.float32
            )
            low_out[rows, :] = by_plane(low_sum, word)
            high_out[rows, :] = by_plane(high_sum, word).astype(jnp.bfloat16)
        first += tail.shape[0]


def window_kernel(wires_by_plane, count, side, first_tail, last_tail, wave, *refs):
    sources, refs = refs[:count], refs[count:]
    high_out, low_out, code_out, table_out, near_out, far_out = refs[:6]
    kept = refs[6 : 6 + count - 4]
    front, slots, offset_rows, bad_rows, kernel_taps, words, wide_taps, sems = refs[6 + count - 4 :]
    held = (slots, offset_rows, bad_rows, kernel_taps)
    copies = start_all(
        [*zip(sources[:4], held), (wave.at[:, :LANES], front), *zip(sources[4:], kept)], sems
    )
    for copy in copies[:5]:
        copy.wait()
    fill_table(kernel_taps, wide_taps, table_out)
    groups = front.shape[0] // LANES
    near_out[...] = slots[pl.ds(side[0] * groups, groups), :]
    far_out[...] = slots[pl.ds((1 - side[0]) * groups, groups), :]
    small = (slots, offset_rows, bad_rows)
    outs = (high_out, low_out, code_out)
    filter_window(wires_by_plane, side, front, (first_tail, last_tail), small, table_out, outs, words)
    for copy in copies[5:]:
        copy.wait()


def finish_early(halo, code, table, low_main, write):
    step = STEP

    def body(i, carry):
        rows = pl.ds(pl.multiple_of(i * step, step), step)
        word = code[rows, :]
        source, wrapped = delays(word)
        early = take_lanes(halo[rows, :].astype(jnp.float32), source)
        both = jnp.concatenate([early, jnp.where(wrapped, early, 0.0)], 1).astype(jnp.bfloat16)
        sums = jnp.dot(both, table[...], preferred_element_type=jnp.float32)
        write(rows, (low_main[rows, :] + by_plane(sums, word)).astype(jnp.bfloat16))
        return carry

    lax.fori_loop(0, halo.shape[0] // step, body, 0, unroll=True)


def other_kernel(first, side, halo, table, high, low_main, code, out):
    rows = pl.ds(first, out.shape[0])

    @pl.when(side[0] == 0)
    def _():
        out[...] = high[rows, :]

    @pl.when(side[0] != 0)
    def _():
        def write(here, value):
            out[here, :] = value

        finish_early(halo, code.at[rows], table, low_main.at[rows], write)


def finish_own(side, halo, table, high, low_main, code, wide):
    @pl.when(side[0] == 0)
    def _():
        def write(rows, value):
            wide[rows, :] = value.astype(jnp.float32)

        finish_early(halo, code, table, low_main, write)

    @pl.when(side[0] != 0)
    def _():
        wide[0 : high.shape[0], :] = high[...].astype(jnp.float32)


def place_rows(count, wide, slots, first, target):
    for k in range(count):
        slot = slots[(first + k) // LANES, (first + k) % LANES]
        target[pl.ds(slot, 1), :] = wide[k : k + 1, :]


def middle_kernel(side, near, far, other, halo, table, high, low_main, code, target, *refs):
    wide, wide_other, near_slots, far_slots, sems = refs
    loads = start_all([(near, near_slots), (far, far_slots)], sems)
    count = halo.shape[0]
    wide_other[...] = other[...].astype(jnp.float32)
    finish_own(side, halo, table, high.at[pl.ds(0, count)], low_main, code, wide)
    for load in loads:
        load.wait()
    place_rows(count, wide_other, far_slots, 0, target)
    place_rows(count, wide, near_slots, 0, target)


def final_kernel(layout, first, side, near, far, other, halo, table, high, low_main, code, before, *refs):
    responses, out, ordered = refs[:3], refs[3], refs[4]
    wide, wide_other, mixed, near_slots, far_slots, sems = refs[5:]
    del before
    own = pl.ds(first, halo.shape[0])
    high, low_main, code = high.at[own], low_main.at[own], code.at[own]
    loads = [
        pltpu.make_async_copy(near, near_slots, sems.at[0]),
        pltpu.make_async_copy(far, far_slots, sems.at[1]),
    ]
    for load in loads:
        load.start()
    wide_other[...] = other[...].astype(jnp.float32)
    finish_own(side, halo, table, high, low_main, code, wide)
    for load in loads:
        load.wait()
    place_rows(other.shape[0], wide_other, far_slots, first, ordered)
    place_rows(halo.shape[0], wide, near_slots, first, ordered)
    copies = []
    for (start, wires), resp in zip(layout, responses):
        half = wires // 2
        base = padded(half)
        front = ordered[start : start + half, :]
        back = ordered[start + half : start + wires, :]
        total = (front + back).astype(jnp.bfloat16)
        change = (front - back).astype(jnp.bfloat16)
        for block in range(base // LANES):
            valid = min(LANES, half - block * LANES)
            columns = slice(base - block * LANES, base - block * LANES + half)
            even = jnp.dot(resp[:valid, columns], total, preferred_element_type=jnp.float32)
            odd = jnp.dot(
                resp[LANES : LANES + valid, columns], change, preferred_element_type=jnp.float32
            )
            top = start + block * LANES
            mixed[top : top + valid, :] = even + odd
            mixed[top + half : top + half + valid, :] = even - odd
        span = pl.ds(start, wires)
        copies.append(pltpu.make_async_copy(mixed.at[span], out.at[span], sems.at[2 + len(copies)]))
        copies[-1].start()
    for copy in copies:
        copy.wait()


def deconvolve(
    waveforms,
    time_kernel,
    wire_slot,
    tick_offset,
    bad_channel,
    induction_real,
    induction_imaginary,
    induction_filter,
    collection_real,
    collection_imaginary,
    collection_filter,
):
    induction = induction_real.shape[1]
    collection = collection_real.shape[0]
    wires_by_plane = (induction, induction, collection)
    taps = time_kernel.shape[1]
    rows, ticks = waveforms.shape
    channels = wire_slot.shape[0]
    assert ticks == 2 * LANES and taps + OFFSET_RANGE == LANES
    assert channels == 2 * rows and channels == 2 * induction + collection
    parts = (rows - LAST_ROWS, LAST_ROWS)

    vm = pl.BlockSpec(memory_space=VMEM)
    sm = pl.BlockSpec(memory_space=SMEM)
    hbm = pl.BlockSpec(memory_space=pltpu.HBM)
    keep = functools.partial(pltpu.with_memory_space_constraint, memory_space=pltpu.HBM)
    shape = jax.ShapeDtypeStruct
    side = lax.axis_index("apa")
    side_word = side.reshape(1).astype(jnp.int32)

    def call(kernel, outs, operands, specs, scratch, flops, **more):
        return pl.pallas_call(
            kernel,
            out_shape=outs,
            in_specs=specs,
            out_specs=more.pop("out_specs", [vm] * len(outs)),
            scratch_shapes=scratch,
            compiler_params=pltpu.CompilerParams(vmem_limit_bytes=KERNEL_VMEM),
            cost_estimate=pl.CostEstimate(flops=flops, bytes_accessed=10**6, transcendentals=0),
            **more,
        )(*operands)

    def by_lanes(vector):
        return vector.reshape(channels // LANES, LANES)

    def like(array):
        return shape(array.shape, array.dtype)

    small = [
        by_lanes(wire_slot),
        by_lanes(tick_offset),
        by_lanes(bad_channel),
        time_kernel,
        induction_real,
        induction_imaginary,
        induction_filter,
        collection_real[None],
        collection_imaginary[None],
        collection_filter[None],
    ]
    first_tail, last_tail = call(
        cut_kernel,
        [shape((count, LANES), waveforms.dtype) for count in parts],
        [keep(waveforms)],
        [hbm],
        [pltpu.SemaphoreType.DMA((2,))],
        10**5,
    )

    groups, ring = lax.axis_size("grp"), lax.axis_size("tm")
    axes = ("grp", "tm", "apa")

    def onward(core):
        pairs = []
        for g in range(groups):
            for t in range(ring):
                here = 2 * (g * ring + t)
                pairs.append((here + core, 2 * (g * ring + (t + 1) % ring) + core))
                pairs.append((here + 1 - core, 2 * ((g + 1) % groups * ring + t) + 1 - core))
        return pairs

    halos = {}
    for name, part in (("first", first_tail), ("last", last_tail)):
        for core, whose in ((1, "other"), (0, "own")):
            halos[whose, name] = lax.ppermute(part, axes, onward(core))

    constants = [jnp.asarray(t) for t in wire_tables(wires_by_plane)]
    sources = [*small, *constants]
    slot_shape = shape((rows // LANES, LANES), jnp.int32)
    window = call(
        functools.partial(window_kernel, wires_by_plane, len(sources)),
        [
            shape((rows, LANES), jnp.bfloat16),
            shape((rows, LANES), jnp.float32),
            shape((rows, LANES), jnp.int32),
            shape((2 * LANES, 3 * LANES), jnp.bfloat16),
            slot_shape,
            slot_shape,
        ]
        + [like(x) for x in sources[4:]],
        [side_word, first_tail, last_tail, *map(keep, [waveforms, *sources])],
        [sm, vm, vm] + [hbm] * (1 + len(sources)),
        [pltpu.VMEM((rows, LANES), jnp.bfloat16)]
        + [pltpu.VMEM(x.shape, x.dtype) for x in small[:4]]
        + [
            pltpu.VMEM((channels // LANES, LANES), jnp.int32),
            pltpu.VMEM((8, LANES), jnp.float32),
            pltpu.SemaphoreType.DMA((1 + len(sources),)),
        ],
        10**9,
    )
    own_part = window[:3]
    table, near, far = window[3:6]
    responses = call(
        functools.partial(response_kernel, wires_by_plane),
        [shape((2 * LANES, 2 * padded(w // 2)), jnp.bfloat16) for w in wires_by_plane],
        list(window[6:]),
        [vm] * 8,
        [],
        10**9,
    )

    received = []
    for name, first in (("first", 0), ("last", parts[0])):
        halo = halos["other", name]
        (other,) = call(
            functools.partial(other_kernel, first),
            [shape(halo.shape, halo.dtype)],
            [side_word, halo, table, *own_part],
            [sm] + [vm] * 5,
            [],
            10**8,
        )
        received.append(lax.ppermute(other, "apa", [(0, 1), (1, 0)]))
    (placed,) = call(
        middle_kernel,
        [shape((channels, LANES), jnp.float32)],
        [side_word, near, far, received[0], halos["own", "first"], table, *own_part],
        [sm] + [vm] * 8,
        [
            pltpu.VMEM((parts[0], LANES), jnp.float32),
            pltpu.VMEM((parts[0], LANES), jnp.float32),
            pltpu.SMEM(slot_shape.shape, jnp.int32),
            pltpu.SMEM(slot_shape.shape, jnp.int32),
            pltpu.SemaphoreType.DMA((2,)),
        ],
        10**8,
    )

    layout = []
    start = 0
    for wires in wires_by_plane:
        layout.append((start, wires))
        start += wires
    return call(
        functools.partial(final_kernel, layout, parts[0]),
        [shape((channels, LANES), jnp.float32)] * 2,
        [side_word, near, far, received[1], halos["own", "last"], table, *own_part, placed, *responses],
        [sm] + [vm] * 12,
        [
            pltpu.VMEM((parts[1], LANES), jnp.float32),
            pltpu.VMEM((parts[1], LANES), jnp.float32),
            pltpu.VMEM((channels, LANES), jnp.float32),
            pltpu.SMEM(slot_shape.shape, jnp.int32),
            pltpu.SMEM(slot_shape.shape, jnp.int32),
            pltpu.SemaphoreType.DMA((5,)),
        ],
        10**9,
        out_specs=[pl.BlockSpec(memory_space=pl.ANY), vm],
        input_output_aliases={9: 1},
    )[0]


def solution(mesh):
    placed = (P(("grp", "apa"), "tm"), P(), P("grp"), P("grp"), P("grp")) + (P(),) * 6
    return jax.shard_map(
        deconvolve, mesh=mesh, in_specs=placed, out_specs=P("grp", ("tm", "apa")), check_vma=False
    )
```

```python
import functools
import math

import jax
import jax.numpy as jnp
import numpy as np
from jax import lax
from jax.experimental import pallas as pl
from jax.experimental.pallas import tpu as pltpu
from jax.sharding import PartitionSpec as P


OFFSET_RANGE = 64
LANES = 128
VMEM = pltpu.VMEM
SMEM = pltpu.SMEM
KERNEL_VMEM = 16 * 2**20
STEP = 256
LAST_ROWS = 384


def padded(count):
    return -(-count // LANES) * LANES


def wire_tables(wires_by_plane):
    widest = max(wires_by_plane)
    coarse_rows, fine_rows = [], []
    for wires in wires_by_plane[1:]:
        base = padded(wires // 2)
        m = np.arange(wires, dtype=np.int64)
        step = np.arange(2 * base // LANES, dtype=np.int64)[:, None] * LANES - base
        turn = 2.0 * math.pi / wires
        coarse = step * m[None, :] % wires * turn
        fine = m[:, None] * np.arange(LANES, dtype=np.int64)[None, :] % wires * turn
        for table in (np.cos(coarse), np.sin(coarse)):
            full = np.zeros((2, step.shape[0], widest), np.float32)
            full[0, :, :wires:2] = table[:, ::2]
            full[1, :, 1:wires:2] = table[:, 1::2]
            coarse_rows.append(full.reshape(-1, widest))
        fine_rows.append(np.concatenate([np.cos(fine), np.sin(fine)], 1).astype(np.float32))
    fine = np.concatenate(fine_rows, 0)
    high = fine.astype(jnp.bfloat16)
    low = (fine - high.astype(np.float32)).astype(jnp.bfloat16)
    return np.concatenate(coarse_rows, 0), np.concatenate([high, low], 1)


def take_lanes(rows, lanes):
    return lax.gather(
        rows,
        lanes[..., None],
        lax.GatherDimensionNumbers(
            offset_dims=(),
            collapsed_slice_dims=(1,),
            start_index_map=(1,),
            operand_batching_dims=(0,),
            start_indices_batching_dims=(0,),
        ),
        slice_sizes=(1, 1),
        mode=lax.GatherScatterMode.PROMISE_IN_BOUNDS,
    )


def lane_roll(row, rows):
    r = lax.broadcasted_iota(jnp.int32, (rows, LANES), 0)
    l = lax.broadcasted_iota(jnp.int32, (rows, LANES), 1)
    return take_lanes(jnp.broadcast_to(row, (rows, LANES)), (l - r) & (LANES - 1))


def split_dot(left, high, low):
    upper = left.astype(jnp.bfloat16)
    lower = (left - upper.astype(jnp.float32)).astype(jnp.bfloat16)
    rows = left.shape[0]
    both = jnp.dot(
        jnp.concatenate([upper, lower], 0), high, preferred_element_type=jnp.float32
    )
    return both[:rows] + both[rows:] + jnp.dot(upper, low, preferred_element_type=jnp.float32)


def make_responses(wires_by_plane, induction, collection, coarse, fine, outs):
    r = lax.broadcasted_iota(jnp.int32, (LANES, LANES), 0)
    l = lax.broadcasted_iota(jnp.int32, (LANES, LANES), 1)
    for plane, wires in enumerate(wires_by_plane):
        out = outs[plane]
        spans = out.shape[1] // LANES
        first = 0 if plane < 2 else coarse.shape[0] - 4 * spans
        ca = coarse[first : first + 2 * spans, :wires]
        sa = coarse[first + 2 * spans : first + 4 * spans, :wires]
        first = 0 if plane < 2 else wires_by_plane[0]
        rows = slice(first, first + wires)
        if plane < 2:
            real, imag, gain = (ref[plane : plane + 1, :] for ref in induction)
        else:
            real, imag, gain = (ref[...] for ref in collection)
        scale = gain / (real * real + imag * imag) * (1.0 / wires)
        ratio_re = real * scale
        ratio_im = -imag * scale
        u = ca * ratio_re + sa * ratio_im
        v = ca * ratio_im - sa * ratio_re
        taps = split_dot(u, fine[rows, :LANES], fine[rows, 2 * LANES : 3 * LANES])
        taps = taps + split_dot(v, fine[rows, LANES : 2 * LANES], fine[rows, 3 * LANES :])
        for parity in range(2):
            top = slice(parity * LANES, (parity + 1) * LANES)
            previous = None
            for span in range(spans):
                row = parity * spans + span
                here = lane_roll(taps[row : row + 1, :], LANES)
                before = here if previous is None else previous
                out[top, span * LANES : (span + 1) * LANES] = jnp.where(l >= r, here, before).astype(
                    jnp.bfloat16
                )
                previous = here


def delays(word):
    lane = lax.broadcasted_iota(jnp.int32, word.shape, 1)
    source = (lane - word) & (LANES - 1)
    return source, source > lane


def by_plane(sums, word):
    picked = jnp.where(word < 3 * LANES, sums[:, 2 * LANES :], 0.0)
    picked = jnp.where(word < 2 * LANES, sums[:, LANES : 2 * LANES], picked)
    return jnp.where(word < LANES, sums[:, :LANES], picked)


def start_all(pairs, sems):
    copies = [
        pltpu.make_async_copy(source, target, sems.at[i])
        for i, (source, target) in enumerate(pairs)
    ]
    for copy in copies:
        copy.start()
    return copies


def cut_kernel(wave, *refs):
    tails, sems = refs[:-1], refs[-1]
    pairs = []
    first = 0
    for tail in tails:
        pairs.append((wave.at[pl.ds(first, tail.shape[0]), LANES:], tail))
        first += tail.shape[0]
    for copy in start_all(pairs, sems):
        copy.wait()


def response_kernel(wires_by_plane, *refs):
    make_responses(wires_by_plane, refs[0:3], refs[3:6], refs[6], refs[7], refs[8:11])


def fill_table(kernel_taps, wide_taps, table_out):
    r = lax.broadcasted_iota(jnp.int32, (LANES, LANES), 0)
    l = lax.broadcasted_iota(jnp.int32, (LANES, LANES), 1)
    wide_taps[...] = jnp.zeros_like(wide_taps)
    wide_taps[0:3, 0 : kernel_taps.shape[1]] = kernel_taps[...].astype(jnp.float32)
    for plane in range(3):
        rolled = lane_roll(wide_taps[plane : plane + 1, :], LANES)
        cols = slice(plane * LANES, (plane + 1) * LANES)
        table_out[:LANES, cols] = jnp.where(l < r, rolled, 0.0).astype(jnp.bfloat16)
        table_out[LANES:, cols] = jnp.where(l >= r, rolled, 0.0).astype(jnp.bfloat16)


def filter_window(wires_by_plane, side, front, tails, small, table, outs, words):
    high_out, low_out, code_out = outs
    slots, offset_rows, bad_rows = small
    one, two = wires_by_plane[0], wires_by_plane[0] + wires_by_plane[1]
    slot = slots[...]
    planes = (slot >= one).astype(jnp.int32) + (slot >= two).astype(jnp.int32)
    planes = jnp.where(bad_rows[...] == 0, planes, 3)
    words[...] = offset_rows[...] + LANES * planes
    groups = front.shape[0] // LANES
    for i in range(groups):
        row = jnp.broadcast_to(words[pl.ds(side[0] * groups + i, 1), :], (LANES, LANES))
        code_out[i * LANES : (i + 1) * LANES, :] = row.T

    first = 0
    for tail in tails:
        step = math.gcd(tail.shape[0], STEP)
        for top in range(0, tail.shape[0], step):
            rows = slice(first + top, first + top + step)
            word = code_out[rows, :]
            source, wrapped = delays(word)
            early = take_lanes(front[rows, :].astype(jnp.float32), source)
            late = take_lanes(tail[top : top + step, :].astype(jnp.float32), source)
            low = jnp.where(wrapped, 0.0, early).astype(jnp.bfloat16)
            both = jnp.concatenate([early, jnp.where(wrapped, early, late)], 1)
            low_sum = jnp.dot(low, table[LANES:, :], preferred_element_type=jnp.float32)
            high_sum = jnp.dot(
                both.astype(jnp.bfloat16), table[...], preferred_element_type=jnp.float32
            )
            low_out[rows, :] = by_plane(low_sum, word)
            high_out[rows, :] = by_plane(high_sum, word).astype(jnp.bfloat16)
        first += tail.shape[0]


def window_kernel(wires_by_plane, count, side, first_tail, last_tail, wave, *refs):
    sources, refs = refs[:count], refs[count:]
    high_out, low_out, code_out, table_out, near_out, far_out = refs[:6]
    kept = refs[6 : 6 + count - 4]
    front, slots, offset_rows, bad_rows, kernel_taps, words, wide_taps, sems = refs[6 + count - 4 :]
    held = (slots, offset_rows, bad_rows, kernel_taps)
    copies = start_all(
        [*zip(sources[:4], held), (wave.at[:, :LANES], front), *zip(sources[4:], kept)], sems
    )
    for copy in copies[:5]:
        copy.wait()
    fill_table(kernel_taps, wide_taps, table_out)
    groups = front.shape[0] // LANES
    near_out[...] = slots[pl.ds(side[0] * groups, groups), :]
    far_out[...] = slots[pl.ds((1 - side[0]) * groups, groups), :]
    small = (slots, offset_rows, bad_rows)
    outs = (high_out, low_out, code_out)
    filter_window(wires_by_plane, side, front, (first_tail, last_tail), small, table_out, outs, words)
    for copy in copies[5:]:
        copy.wait()


def finish_early(halo, code, table, low_main, write):
    step = math.gcd(halo.shape[0], STEP)

    def body(i, carry):
        rows = pl.ds(pl.multiple_of(i * step, step), step)
        word = code[rows, :]
        source, wrapped = delays(word)
        early = take_lanes(halo[rows, :].astype(jnp.float32), source)
        both = jnp.concatenate([early, jnp.where(wrapped, early, 0.0)], 1).astype(jnp.bfloat16)
        sums = jnp.dot(both, table[...], preferred_element_type=jnp.float32)
        write(rows, (low_main[rows, :] + by_plane(sums, word)).astype(jnp.bfloat16))
        return carry

    lax.fori_loop(0, halo.shape[0] // step, body, 0, unroll=True)


def other_kernel(first, side, halo, table, high, low_main, code, out):
    rows = pl.ds(first, out.shape[0])

    @pl.when(side[0] == 0)
    def _():
        out[...] = high[rows, :]

    @pl.when(side[0] != 0)
    def _():
        def write(here, value):
            out[here, :] = value

        finish_early(halo, code.at[rows], table, low_main.at[rows], write)


def finish_own(side, halo, table, high, low_main, code, wide):
    @pl.when(side[0] == 0)
    def _():
        def write(rows, value):
            wide[rows, :] = value.astype(jnp.float32)

        finish_early(halo, code, table, low_main, write)

    @pl.when(side[0] != 0)
    def _():
        wide[0 : high.shape[0], :] = high[...].astype(jnp.float32)


def place_rows(count, wide, slots, first, target):
    for k in range(count):
        slot = slots[(first + k) // LANES, (first + k) % LANES]
        target[pl.ds(slot, 1), :] = wide[k : k + 1, :]


def place_kernel(far, other, target, wide, slots, sem):
    copy = pltpu.make_async_copy(far, slots, sem.at[0])
    copy.start()
    wide[...] = other[...].astype(jnp.float32)
    copy.wait()
    place_rows(other.shape[0], wide, slots, 0, target)


def own_kernel(side, near, halo, table, high, low_main, code, before, target, wide, slots, sem):
    del before
    copy = pltpu.make_async_copy(near, slots, sem.at[0])
    copy.start()
    finish_own(side, halo, table, high.at[pl.ds(0, halo.shape[0])], low_main, code, wide)
    copy.wait()
    place_rows(halo.shape[0], wide, slots, 0, target)


def final_kernel(layout, first, side, near, far, other, halo, table, high, low_main, code, before, *refs):
    responses, out, ordered = refs[:3], refs[3], refs[4]
    wide, wide_other, mixed, near_slots, far_slots, sems = refs[5:]
    del before
    own = pl.ds(first, halo.shape[0])
    high, low_main, code = high.at[own], low_main.at[own], code.at[own]
    loads = [
        pltpu.make_async_copy(near, near_slots, sems.at[0]),
        pltpu.make_async_copy(far, far_slots, sems.at[1]),
    ]
    for load in loads:
        load.start()
    wide_other[...] = other[...].astype(jnp.float32)
    finish_own(side, halo, table, high, low_main, code, wide)
    for load in loads:
        load.wait()
    place_rows(other.shape[0], wide_other, far_slots, first, ordered)
    place_rows(halo.shape[0], wide, near_slots, first, ordered)
    copies = []
    for (start, wires), resp in zip(layout, responses):
        half = wires // 2
        base = padded(half)
        front = ordered[start : start + half, :]
        back = ordered[start + half : start + wires, :]
        total = (front + back).astype(jnp.bfloat16)
        change = (front - back).astype(jnp.bfloat16)
        for block in range(base // LANES):
            valid = min(LANES, half - block * LANES)
            columns = slice(base - block * LANES, base - block * LANES + half)
            even = jnp.dot(resp[:valid, columns], total, preferred_element_type=jnp.float32)
            odd = jnp.dot(
                resp[LANES : LANES + valid, columns], change, preferred_element_type=jnp.float32
            )
            top = start + block * LANES
            mixed[top : top + valid, :] = even + odd
            mixed[top + half : top + half + valid, :] = even - odd
        span = pl.ds(start, wires)
        copies.append(pltpu.make_async_copy(mixed.at[span], out.at[span], sems.at[2 + len(copies)]))
        copies[-1].start()
    for copy in copies:
        copy.wait()


def deconvolve(
    waveforms,
    time_kernel,
    wire_slot,
    tick_offset,
    bad_channel,
    induction_real,
    induction_imaginary,
    induction_filter,
    collection_real,
    collection_imaginary,
    collection_filter,
):
    induction = induction_real.shape[1]
    collection = collection_real.shape[0]
    wires_by_plane = (induction, induction, collection)
    taps = time_kernel.shape[1]
    rows, ticks = waveforms.shape
    channels = wire_slot.shape[0]
    assert ticks == 2 * LANES and taps + OFFSET_RANGE == LANES
    assert channels == 2 * rows and channels == 2 * induction + collection
    parts = (rows - LAST_ROWS, LAST_ROWS)

    vm = pl.BlockSpec(memory_space=VMEM)
    sm = pl.BlockSpec(memory_space=SMEM)
    hbm = pl.BlockSpec(memory_space=pltpu.HBM)
    keep = functools.partial(pltpu.with_memory_space_constraint, memory_space=pltpu.HBM)
    shape = jax.ShapeDtypeStruct
    side = lax.axis_index("apa")
    side_word = side.reshape(1).astype(jnp.int32)

    def call(kernel, outs, operands, specs, scratch, flops, **more):
        return pl.pallas_call(
            kernel,
            out_shape=outs,
            in_specs=specs,
            out_specs=more.pop("out_specs", [vm] * len(outs)),
            scratch_shapes=scratch,
            compiler_params=pltpu.CompilerParams(vmem_limit_bytes=KERNEL_VMEM),
            cost_estimate=pl.CostEstimate(flops=flops, bytes_accessed=10**6, transcendentals=0),
            **more,
        )(*operands)

    def by_lanes(vector):
        return vector.reshape(channels // LANES, LANES)

    def like(array):
        return shape(array.shape, array.dtype)

    small = [
        by_lanes(wire_slot),
        by_lanes(tick_offset),
        by_lanes(bad_channel),
        time_kernel,
        induction_real,
        induction_imaginary,
        induction_filter,
        collection_real[None],
        collection_imaginary[None],
        collection_filter[None],
    ]
    first_tail, last_tail = call(
        cut_kernel,
        [shape((count, LANES), waveforms.dtype) for count in parts],
        [keep(waveforms)],
        [hbm],
        [pltpu.SemaphoreType.DMA((2,))],
        10**5,
    )

    groups, ring = lax.axis_size("grp"), lax.axis_size("tm")
    axes = ("grp", "tm", "apa")

    def onward(core):
        pairs = []
        for g in range(groups):
            for t in range(ring):
                here = 2 * (g * ring + t)
                pairs.append((here + core, 2 * (g * ring + (t + 1) % ring) + core))
                pairs.append((here + 1 - core, 2 * ((g + 1) % groups * ring + t) + 1 - core))
        return pairs

    halos = {}
    for name, part in (("first", first_tail), ("last", last_tail)):
        for core, whose in ((1, "other"), (0, "own")):
            halos[whose, name] = lax.ppermute(part, axes, onward(core))

    constants = [jnp.asarray(t) for t in wire_tables(wires_by_plane)]
    sources = [*small, *constants]
    slot_shape = shape((rows // LANES, LANES), jnp.int32)
    window = call(
        functools.partial(window_kernel, wires_by_plane, len(sources)),
        [
            shape((rows, LANES), jnp.bfloat16),
            shape((rows, LANES), jnp.float32),
            shape((rows, LANES), jnp.int32),
            shape((2 * LANES, 3 * LANES), jnp.bfloat16),
            slot_shape,
            slot_shape,
        ]
        + [like(x) for x in sources[4:]],
        [side_word, first_tail, last_tail, *map(keep, [waveforms, *sources])],
        [sm, vm, vm] + [hbm] * (1 + len(sources)),
        [pltpu.VMEM((rows, LANES), jnp.bfloat16)]
        + [pltpu.VMEM(x.shape, x.dtype) for x in small[:4]]
        + [
            pltpu.VMEM((channels // LANES, LANES), jnp.int32),
            pltpu.VMEM((8, LANES), jnp.float32),
            pltpu.SemaphoreType.DMA((1 + len(sources),)),
        ],
        10**9,
    )
    own_part = window[:3]
    table, near, far = window[3:6]
    responses = call(
        functools.partial(response_kernel, wires_by_plane),
        [shape((2 * LANES, 2 * padded(w // 2)), jnp.bfloat16) for w in wires_by_plane],
        list(window[6:]),
        [vm] * 8,
        [],
        10**9,
    )

    received = []
    for name, first in (("first", 0), ("last", parts[0])):
        halo = halos["other", name]
        (other,) = call(
            functools.partial(other_kernel, first),
            [shape(halo.shape, halo.dtype)],
            [side_word, halo, table, *own_part],
            [sm] + [vm] * 5,
            [],
            10**8,
        )
        received.append(lax.ppermute(other, "apa", [(0, 1), (1, 0)]))
    placing = [
        pltpu.VMEM((parts[0], LANES), jnp.float32),
        pltpu.SMEM(slot_shape.shape, jnp.int32),
        pltpu.SemaphoreType.DMA((1,)),
    ]
    (placed,) = call(
        place_kernel,
        [shape((channels, LANES), jnp.float32)],
        [far, received[0]],
        [vm] * 2,
        placing,
        10**8,
    )
    (placed,) = call(
        own_kernel,
        [shape((channels, LANES), jnp.float32)],
        [side_word, near, halos["own", "first"], table, *own_part, placed],
        [sm] + [vm] * 7,
        placing,
        10**8,
        input_output_aliases={7: 0},
    )

    layout = []
    start = 0
    for wires in wires_by_plane:
        layout.append((start, wires))
        start += wires
    return call(
        functools.partial(final_kernel, layout, parts[0]),
        [shape((channels, LANES), jnp.float32)] * 2,
        [side_word, near, far, received[1], halos["own", "last"], table, *own_part, placed, *responses],
        [sm] + [vm] * 12,
        [
            pltpu.VMEM((parts[1], LANES), jnp.float32),
            pltpu.VMEM((parts[1], LANES), jnp.float32),
            pltpu.VMEM((channels, LANES), jnp.float32),
            pltpu.SMEM(slot_shape.shape, jnp.int32),
            pltpu.SMEM(slot_shape.shape, jnp.int32),
            pltpu.SemaphoreType.DMA((5,)),
        ],
        10**9,
        out_specs=[pl.BlockSpec(memory_space=pl.ANY), vm],
        input_output_aliases={9: 1},
    )[0]


def solution(mesh):
    placed = (P(("grp", "apa"), "tm"), P(), P("grp"), P("grp"), P("grp")) + (P(),) * 6
    return jax.shard_map(
        deconvolve, mesh=mesh, in_specs=placed, out_specs=P("grp", ("tm", "apa")), check_vma=False
    )
```

```python
import functools
import math

import jax
import jax.numpy as jnp
import numpy as np
from jax import lax
from jax.experimental import pallas as pl
from jax.experimental.pallas import tpu as pltpu
from jax.sharding import PartitionSpec as P


OFFSET_RANGE = 64
LANES = 128
VMEM = pltpu.VMEM
SMEM = pltpu.SMEM
KERNEL_VMEM = 16 * 2**20
BLOCKS = (448, 384, 320, 256, 128)
LAST_ROWS = 384


def block_rows(count):
    return next(size for size in BLOCKS if count % size == 0)


def padded(count):
    return -(-count // LANES) * LANES


def wire_tables(wires_by_plane):
    widest = max(wires_by_plane)
    coarse_rows, fine_rows = [], []
    for wires in wires_by_plane[1:]:
        base = padded(wires // 2)
        m = np.arange(wires, dtype=np.int64)
        step = np.arange(2 * base // LANES, dtype=np.int64)[:, None] * LANES - base
        turn = 2.0 * math.pi / wires
        coarse = step * m[None, :] % wires * turn
        fine = m[:, None] * np.arange(LANES, dtype=np.int64)[None, :] % wires * turn
        for table in (np.cos(coarse), np.sin(coarse)):
            full = np.zeros((2, step.shape[0], widest), np.float32)
            full[0, :, :wires:2] = table[:, ::2]
            full[1, :, 1:wires:2] = table[:, 1::2]
            coarse_rows.append(full.reshape(-1, widest))
        fine_rows.append(np.concatenate([np.cos(fine), np.sin(fine)], 1).astype(np.float32))
    fine = np.concatenate(fine_rows, 0)
    high = fine.astype(jnp.bfloat16)
    low = (fine - high.astype(np.float32)).astype(jnp.bfloat16)
    return np.concatenate(coarse_rows, 0), np.concatenate([high, low], 1)


def take_lanes(rows, lanes):
    return lax.gather(
        rows,
        lanes[..., None],
        lax.GatherDimensionNumbers(
            offset_dims=(),
            collapsed_slice_dims=(1,),
            start_index_map=(1,),
            operand_batching_dims=(0,),
            start_indices_batching_dims=(0,),
        ),
        slice_sizes=(1, 1),
        mode=lax.GatherScatterMode.PROMISE_IN_BOUNDS,
    )


def lane_roll(row, rows):
    r = lax.broadcasted_iota(jnp.int32, (rows, LANES), 0)
    l = lax.broadcasted_iota(jnp.int32, (rows, LANES), 1)
    return take_lanes(jnp.broadcast_to(row, (rows, LANES)), (l - r) & (LANES - 1))


def split_dot(left, high, low):
    upper = left.astype(jnp.bfloat16)
    lower = (left - upper.astype(jnp.float32)).astype(jnp.bfloat16)
    rows = left.shape[0]
    both = jnp.dot(
        jnp.concatenate([upper, lower], 0), high, preferred_element_type=jnp.float32
    )
    return both[:rows] + both[rows:] + jnp.dot(upper, low, preferred_element_type=jnp.float32)


def make_responses(wires_by_plane, induction, collection, coarse, fine, outs):
    r = lax.broadcasted_iota(jnp.int32, (LANES, LANES), 0)
    l = lax.broadcasted_iota(jnp.int32, (LANES, LANES), 1)
    for plane, wires in enumerate(wires_by_plane):
        out = outs[plane]
        spans = out.shape[1] // LANES
        first = 0 if plane < 2 else coarse.shape[0] - 4 * spans
        ca = coarse[first : first + 2 * spans, :wires]
        sa = coarse[first + 2 * spans : first + 4 * spans, :wires]
        first = 0 if plane < 2 else wires_by_plane[0]
        rows = slice(first, first + wires)
        if plane < 2:
            real, imag, gain = (ref[plane : plane + 1, :] for ref in induction)
        else:
            real, imag, gain = (ref[...] for ref in collection)
        scale = gain / (real * real + imag * imag) * (1.0 / wires)
        ratio_re = real * scale
        ratio_im = -imag * scale
        u = ca * ratio_re + sa * ratio_im
        v = ca * ratio_im - sa * ratio_re
        taps = split_dot(u, fine[rows, :LANES], fine[rows, 2 * LANES : 3 * LANES])
        taps = taps + split_dot(v, fine[rows, LANES : 2 * LANES], fine[rows, 3 * LANES :])
        for parity in range(2):
            top = slice(parity * LANES, (parity + 1) * LANES)
            previous = None
            for span in range(spans):
                row = parity * spans + span
                here = lane_roll(taps[row : row + 1, :], LANES)
                before = here if previous is None else previous
                out[top, span * LANES : (span + 1) * LANES] = jnp.where(l >= r, here, before).astype(
                    jnp.bfloat16
                )
                previous = here


def delays(word):
    lane = lax.broadcasted_iota(jnp.int32, word.shape, 1)
    source = (lane - word) & (LANES - 1)
    return source, source > lane


def by_plane(sums, word):
    picked = jnp.where(word < 3 * LANES, sums[:, 2 * LANES :], 0.0)
    picked = jnp.where(word < 2 * LANES, sums[:, LANES : 2 * LANES], picked)
    return jnp.where(word < LANES, sums[:, :LANES], picked)


def start_all(pairs, sems):
    copies = [
        pltpu.make_async_copy(source, target, sems.at[i])
        for i, (source, target) in enumerate(pairs)
    ]
    for copy in copies:
        copy.start()
    return copies


def cut_kernel(wave, *refs):
    tails, sems = refs[:-1], refs[-1]
    pairs = []
    first = 0
    for tail in tails:
        pairs.append((wave.at[pl.ds(first, tail.shape[0]), LANES:], tail))
        first += tail.shape[0]
    for copy in start_all(pairs, sems):
        copy.wait()


def response_kernel(wires_by_plane, *refs):
    make_responses(wires_by_plane, refs[0:3], refs[3:6], refs[6], refs[7], refs[8:11])


def fill_table(kernel_taps, wide_taps, table_out):
    r = lax.broadcasted_iota(jnp.int32, (LANES, LANES), 0)
    l = lax.broadcasted_iota(jnp.int32, (LANES, LANES), 1)
    wide_taps[...] = jnp.zeros_like(wide_taps)
    wide_taps[0:3, 0 : kernel_taps.shape[1]] = kernel_taps[...].astype(jnp.float32)
    for plane in range(3):
        rolled = lane_roll(wide_taps[plane : plane + 1, :], LANES)
        cols = slice(plane * LANES, (plane + 1) * LANES)
        table_out[:LANES, cols] = jnp.where(l < r, rolled, 0.0).astype(jnp.bfloat16)
        table_out[LANES:, cols] = jnp.where(l >= r, rolled, 0.0).astype(jnp.bfloat16)


def filter_window(wires_by_plane, side, front, tails, small, table, outs, words):
    high_out, low_out, code_out = outs
    slots, offset_rows, bad_rows = small
    one, two = wires_by_plane[0], wires_by_plane[0] + wires_by_plane[1]
    slot = slots[...]
    planes = (slot >= one).astype(jnp.int32) + (slot >= two).astype(jnp.int32)
    planes = jnp.where(bad_rows[...] == 0, planes, 3)
    words[...] = offset_rows[...] + LANES * planes
    groups = front.shape[0] // LANES
    for i in range(groups):
        row = jnp.broadcast_to(words[pl.ds(side[0] * groups + i, 1), :], (LANES, LANES))
        code_out[i * LANES : (i + 1) * LANES, :] = row.T

    first = 0
    for tail in tails:
        step = block_rows(tail.shape[0])
        for top in range(0, tail.shape[0], step):
            rows = slice(first + top, first + top + step)
            word = code_out[rows, :]
            source, wrapped = delays(word)
            early = take_lanes(front[rows, :].astype(jnp.float32), source)
            late = take_lanes(tail[top : top + step, :].astype(jnp.float32), source)
            low = jnp.where(wrapped, 0.0, early).astype(jnp.bfloat16)
            both = jnp.concatenate([early, jnp.where(wrapped, early, late)], 1)
            low_sum = jnp.dot(low, table[LANES:, :], preferred_element_type=jnp.float32)
            high_sum = jnp.dot(
                both.astype(jnp.bfloat16), table[...], preferred_element_type=jnp.float32
            )
            low_out[rows, :] = by_plane(low_sum, word)
            high_out[rows, :] = by_plane(high_sum, word).astype(jnp.bfloat16)
        first += tail.shape[0]


def window_kernel(wires_by_plane, count, side, first_tail, last_tail, wave, *refs):
    sources, refs = refs[:count], refs[count:]
    high_out, low_out, code_out, table_out, near_out, far_out = refs[:6]
    kept = refs[6 : 6 + count - 4]
    front, slots, offset_rows, bad_rows, kernel_taps, words, wide_taps, sems = refs[6 + count - 4 :]
    held = (slots, offset_rows, bad_rows, kernel_taps)
    copies = start_all(
        [*zip(sources[:4], held), (wave.at[:, :LANES], front), *zip(sources[4:], kept)], sems
    )
    for copy in copies[:5]:
        copy.wait()
    fill_table(kernel_taps, wide_taps, table_out)
    groups = front.shape[0] // LANES
    near_out[...] = slots[pl.ds(side[0] * groups, groups), :]
    far_out[...] = slots[pl.ds((1 - side[0]) * groups, groups), :]
    small = (slots, offset_rows, bad_rows)
    outs = (high_out, low_out, code_out)
    filter_window(wires_by_plane, side, front, (first_tail, last_tail), small, table_out, outs, words)
    for copy in copies[5:]:
        copy.wait()


def finish_early(halo, code, table, low_main, write):
    step = block_rows(halo.shape[0])

    def body(i, carry):
        rows = pl.ds(pl.multiple_of(i * step, step), step)
        word = code[rows, :]
        source, wrapped = delays(word)
        early = take_lanes(halo[rows, :].astype(jnp.float32), source)
        both = jnp.concatenate([early, jnp.where(wrapped, early, 0.0)], 1).astype(jnp.bfloat16)
        sums = jnp.dot(both, table[...], preferred_element_type=jnp.float32)
        write(rows, (low_main[rows, :] + by_plane(sums, word)).astype(jnp.bfloat16))
        return carry

    lax.fori_loop(0, halo.shape[0] // step, body, 0, unroll=True)


def other_kernel(first, side, halo, table, high, low_main, code, out):
    rows = pl.ds(first, out.shape[0])

    @pl.when(side[0] == 0)
    def _():
        out[...] = high[rows, :]

    @pl.when(side[0] != 0)
    def _():
        def write(here, value):
            out[here, :] = value

        finish_early(halo, code.at[rows], table, low_main.at[rows], write)


def finish_own(side, halo, table, high, low_main, code, wide):
    @pl.when(side[0] == 0)
    def _():
        def write(rows, value):
            wide[rows, :] = value.astype(jnp.float32)

        finish_early(halo, code, table, low_main, write)

    @pl.when(side[0] != 0)
    def _():
        wide[0 : high.shape[0], :] = high[...].astype(jnp.float32)


def place_rows(count, wide, slots, first, target):
    for k in range(count):
        slot = slots[(first + k) // LANES, (first + k) % LANES]
        target[pl.ds(slot, 1), :] = wide[k : k + 1, :]


def place_kernel(far, other, target, wide, slots, sem):
    copy = pltpu.make_async_copy(far, slots, sem.at[0])
    copy.start()
    wide[...] = other[...].astype(jnp.float32)
    copy.wait()
    place_rows(other.shape[0], wide, slots, 0, target)


def own_kernel(side, near, halo, table, high, low_main, code, before, target, wide, slots, sem):
    del before
    copy = pltpu.make_async_copy(near, slots, sem.at[0])
    copy.start()
    finish_own(side, halo, table, high.at[pl.ds(0, halo.shape[0])], low_main, code, wide)
    copy.wait()
    place_rows(halo.shape[0], wide, slots, 0, target)


def final_kernel(layout, first, side, near, far, other, halo, table, high, low_main, code, before, *refs):
    responses, out, ordered = refs[:3], refs[3], refs[4]
    wide, wide_other, mixed, near_slots, far_slots, sems = refs[5:]
    del before
    own = pl.ds(first, halo.shape[0])
    high, low_main, code = high.at[own], low_main.at[own], code.at[own]
    loads = [
        pltpu.make_async_copy(near, near_slots, sems.at[0]),
        pltpu.make_async_copy(far, far_slots, sems.at[1]),
    ]
    for load in loads:
        load.start()
    wide_other[...] = other[...].astype(jnp.float32)
    finish_own(side, halo, table, high, low_main, code, wide)
    for load in loads:
        load.wait()
    place_rows(other.shape[0], wide_other, far_slots, first, ordered)
    place_rows(halo.shape[0], wide, near_slots, first, ordered)
    copies = []
    for (start, wires), resp in zip(layout, responses):
        half = wires // 2
        base = padded(half)
        front = ordered[start : start + half, :]
        back = ordered[start + half : start + wires, :]
        total = (front + back).astype(jnp.bfloat16)
        change = (front - back).astype(jnp.bfloat16)
        sizes = [min(LANES, half - top) for top in range(0, half, LANES)]

        def rows_of(part):
            lefts = [base - block * LANES for block in range(len(sizes))]
            pieces = [
                resp[part * LANES : part * LANES + size, left : left + half]
                for size, left in zip(sizes, lefts)
            ]
            return jnp.concatenate(pieces, 0)

        even = jnp.dot(rows_of(0), total, preferred_element_type=jnp.float32)
        odd = jnp.dot(rows_of(1), change, preferred_element_type=jnp.float32)
        mixed[start : start + half, :] = even + odd
        mixed[start + half : start + wires, :] = even - odd
        span = pl.ds(start, wires)
        copies.append(pltpu.make_async_copy(mixed.at[span], out.at[span], sems.at[2 + len(copies)]))
        copies[-1].start()
    for copy in copies:
        copy.wait()


def deconvolve(
    waveforms,
    time_kernel,
    wire_slot,
    tick_offset,
    bad_channel,
    induction_real,
    induction_imaginary,
    induction_filter,
    collection_real,
    collection_imaginary,
    collection_filter,
):
    induction = induction_real.shape[1]
    collection = collection_real.shape[0]
    wires_by_plane = (induction, induction, collection)
    taps = time_kernel.shape[1]
    rows, ticks = waveforms.shape
    channels = wire_slot.shape[0]
    assert ticks == 2 * LANES and taps + OFFSET_RANGE == LANES
    assert channels == 2 * rows and channels == 2 * induction + collection
    parts = (rows - LAST_ROWS, LAST_ROWS)

    vm = pl.BlockSpec(memory_space=VMEM)
    sm = pl.BlockSpec(memory_space=SMEM)
    hbm = pl.BlockSpec(memory_space=pltpu.HBM)
    keep = functools.partial(pltpu.with_memory_space_constraint, memory_space=pltpu.HBM)
    shape = jax.ShapeDtypeStruct
    side = lax.axis_index("apa")
    side_word = side.reshape(1).astype(jnp.int32)

    def call(kernel, outs, operands, specs, scratch, flops, **more):
        return pl.pallas_call(
            kernel,
            out_shape=outs,
            in_specs=specs,
            out_specs=more.pop("out_specs", [vm] * len(outs)),
            scratch_shapes=scratch,
            compiler_params=pltpu.CompilerParams(vmem_limit_bytes=KERNEL_VMEM),
            cost_estimate=pl.CostEstimate(flops=flops, bytes_accessed=10**6, transcendentals=0),
            **more,
        )(*operands)

    def by_lanes(vector):
        return vector.reshape(channels // LANES, LANES)

    def like(array):
        return shape(array.shape, array.dtype)

    small = [
        by_lanes(wire_slot),
        by_lanes(tick_offset),
        by_lanes(bad_channel),
        time_kernel,
        induction_real,
        induction_imaginary,
        induction_filter,
        collection_real[None],
        collection_imaginary[None],
        collection_filter[None],
    ]
    first_tail, last_tail = call(
        cut_kernel,
        [shape((count, LANES), waveforms.dtype) for count in parts],
        [keep(waveforms)],
        [hbm],
        [pltpu.SemaphoreType.DMA((2,))],
        10**5,
    )

    groups, ring = lax.axis_size("grp"), lax.axis_size("tm")
    axes = ("grp", "tm", "apa")

    def onward(core):
        pairs = []
        for g in range(groups):
            for t in range(ring):
                here = 2 * (g * ring + t)
                pairs.append((here + core, 2 * (g * ring + (t + 1) % ring) + core))
                pairs.append((here + 1 - core, 2 * ((g + 1) % groups * ring + t) + 1 - core))
        return pairs

    halos = {}
    for name, part in (("first", first_tail), ("last", last_tail)):
        for core, whose in ((1, "other"), (0, "own")):
            halos[whose, name] = lax.ppermute(part, axes, onward(core))

    constants = [jnp.asarray(t) for t in wire_tables(wires_by_plane)]
    sources = [*small, *constants]
    slot_shape = shape((rows // LANES, LANES), jnp.int32)
    window = call(
        functools.partial(window_kernel, wires_by_plane, len(sources)),
        [
            shape((rows, LANES), jnp.bfloat16),
            shape((rows, LANES), jnp.float32),
            shape((rows, LANES), jnp.int32),
            shape((2 * LANES, 3 * LANES), jnp.bfloat16),
            slot_shape,
            slot_shape,
        ]
        + [like(x) for x in sources[4:]],
        [side_word, first_tail, last_tail, *map(keep, [waveforms, *sources])],
        [sm, vm, vm] + [hbm] * (1 + len(sources)),
        [pltpu.VMEM((rows, LANES), jnp.bfloat16)]
        + [pltpu.VMEM(x.shape, x.dtype) for x in small[:4]]
        + [
            pltpu.VMEM((channels // LANES, LANES), jnp.int32),
            pltpu.VMEM((8, LANES), jnp.float32),
            pltpu.SemaphoreType.DMA((1 + len(sources),)),
        ],
        10**9,
    )
    own_part = window[:3]
    table, near, far = window[3:6]
    responses = call(
        functools.partial(response_kernel, wires_by_plane),
        [shape((2 * LANES, 2 * padded(w // 2)), jnp.bfloat16) for w in wires_by_plane],
        list(window[6:]),
        [vm] * 8,
        [],
        10**9,
    )

    received = []
    for name, first in (("first", 0), ("last", parts[0])):
        halo = halos["other", name]
        (other,) = call(
            functools.partial(other_kernel, first),
            [shape(halo.shape, halo.dtype)],
            [side_word, halo, table, *own_part],
            [sm] + [vm] * 5,
            [],
            10**8,
        )
        received.append(lax.ppermute(other, "apa", [(0, 1), (1, 0)]))
    placing = [
        pltpu.VMEM((parts[0], LANES), jnp.float32),
        pltpu.SMEM(slot_shape.shape, jnp.int32),
        pltpu.SemaphoreType.DMA((1,)),
    ]
    (placed,) = call(
        place_kernel,
        [shape((channels, LANES), jnp.float32)],
        [far, received[0]],
        [vm] * 2,
        placing,
        10**8,
    )
    (placed,) = call(
        own_kernel,
        [shape((channels, LANES), jnp.float32)],
        [side_word, near, halos["own", "first"], table, *own_part, placed],
        [sm] + [vm] * 7,
        placing,
        10**8,
        input_output_aliases={7: 0},
    )

    layout = []
    start = 0
    for wires in wires_by_plane:
        layout.append((start, wires))
        start += wires
    return call(
        functools.partial(final_kernel, layout, parts[0]),
        [shape((channels, LANES), jnp.float32)] * 2,
        [side_word, near, far, received[1], halos["own", "last"], table, *own_part, placed, *responses],
        [sm] + [vm] * 12,
        [
            pltpu.VMEM((parts[1], LANES), jnp.float32),
            pltpu.VMEM((parts[1], LANES), jnp.float32),
            pltpu.VMEM((channels, LANES), jnp.float32),
            pltpu.SMEM(slot_shape.shape, jnp.int32),
            pltpu.SMEM(slot_shape.shape, jnp.int32),
            pltpu.SemaphoreType.DMA((5,)),
        ],
        10**9,
        out_specs=[pl.BlockSpec(memory_space=pl.ANY), vm],
        input_output_aliases={9: 1},
    )[0]


def solution(mesh):
    placed = (P(("grp", "apa"), "tm"), P(), P("grp"), P("grp"), P("grp")) + (P(),) * 6
    return jax.shard_map(
        deconvolve, mesh=mesh, in_specs=placed, out_specs=P("grp", ("tm", "apa")), check_vma=False
    )
```

```python
import functools
import math

import jax
import jax.numpy as jnp
import numpy as np
from jax import lax
from jax.experimental import pallas as pl
from jax.experimental.pallas import tpu as pltpu
from jax.sharding import PartitionSpec as P


OFFSET_RANGE = 64
LANES = 128
VMEM = pltpu.VMEM
SMEM = pltpu.SMEM
KERNEL_VMEM = 16 * 2**20
BLOCKS = (448, 384, 320, 256, 128)
LAST_ROWS = 384


def block_rows(count):
    return next(size for size in BLOCKS if count % size == 0)


def padded(count):
    return -(-count // LANES) * LANES


def wire_tables(wires_by_plane):
    widest = max(wires_by_plane)
    coarse_rows, fine_rows = [], []
    for wires in wires_by_plane[1:]:
        base = padded(wires // 2)
        m = np.arange(wires, dtype=np.int64)
        step = np.arange(2 * base // LANES, dtype=np.int64)[:, None] * LANES - base
        turn = 2.0 * math.pi / wires
        coarse = step * m[None, :] % wires * turn
        fine = m[:, None] * np.arange(LANES, dtype=np.int64)[None, :] % wires * turn
        for table in (np.cos(coarse), np.sin(coarse)):
            full = np.zeros((2, step.shape[0], widest), np.float32)
            full[0, :, :wires:2] = table[:, ::2]
            full[1, :, 1:wires:2] = table[:, 1::2]
            coarse_rows.append(full.reshape(-1, widest))
        fine_rows.append(np.concatenate([np.cos(fine), np.sin(fine)], 1).astype(np.float32))
    fine = np.concatenate(fine_rows, 0)
    high = fine.astype(jnp.bfloat16)
    low = (fine - high.astype(np.float32)).astype(jnp.bfloat16)
    return np.concatenate(coarse_rows, 0), np.concatenate([high, low], 1)


def take_lanes(rows, lanes):
    return lax.gather(
        rows,
        lanes[..., None],
        lax.GatherDimensionNumbers(
            offset_dims=(),
            collapsed_slice_dims=(1,),
            start_index_map=(1,),
            operand_batching_dims=(0,),
            start_indices_batching_dims=(0,),
        ),
        slice_sizes=(1, 1),
        mode=lax.GatherScatterMode.PROMISE_IN_BOUNDS,
    )


def lane_roll(row, rows):
    r = lax.broadcasted_iota(jnp.int32, (rows, LANES), 0)
    l = lax.broadcasted_iota(jnp.int32, (rows, LANES), 1)
    return take_lanes(jnp.broadcast_to(row, (rows, LANES)), (l - r) & (LANES - 1))


def split_dot(left, high, low):
    upper = left.astype(jnp.bfloat16)
    lower = (left - upper.astype(jnp.float32)).astype(jnp.bfloat16)
    rows = left.shape[0]
    both = jnp.dot(
        jnp.concatenate([upper, lower], 0), high, preferred_element_type=jnp.float32
    )
    return both[:rows] + both[rows:] + jnp.dot(upper, low, preferred_element_type=jnp.float32)


def make_responses(wires_by_plane, induction, collection, coarse, fine, outs):
    r = lax.broadcasted_iota(jnp.int32, (LANES, LANES), 0)
    l = lax.broadcasted_iota(jnp.int32, (LANES, LANES), 1)
    for plane, wires in enumerate(wires_by_plane):
        out = outs[plane]
        spans = out.shape[1] // LANES
        first = 0 if plane < 2 else coarse.shape[0] - 4 * spans
        ca = coarse[first : first + 2 * spans, :wires]
        sa = coarse[first + 2 * spans : first + 4 * spans, :wires]
        first = 0 if plane < 2 else wires_by_plane[0]
        rows = slice(first, first + wires)
        if plane < 2:
            real, imag, gain = (ref[plane : plane + 1, :] for ref in induction)
        else:
            real, imag, gain = (ref[...] for ref in collection)
        scale = gain / (real * real + imag * imag) * (1.0 / wires)
        ratio_re = real * scale
        ratio_im = -imag * scale
        u = ca * ratio_re + sa * ratio_im
        v = ca * ratio_im - sa * ratio_re
        taps = split_dot(u, fine[rows, :LANES], fine[rows, 2 * LANES : 3 * LANES])
        taps = taps + split_dot(v, fine[rows, LANES : 2 * LANES], fine[rows, 3 * LANES :])
        for parity in range(2):
            top = slice(parity * LANES, (parity + 1) * LANES)
            previous = None
            for span in range(spans):
                row = parity * spans + span
                here = lane_roll(taps[row : row + 1, :], LANES)
                before = here if previous is None else previous
                out[top, span * LANES : (span + 1) * LANES] = jnp.where(l >= r, here, before).astype(
                    jnp.bfloat16
                )
                previous = here


def delays(word):
    lane = lax.broadcasted_iota(jnp.int32, word.shape, 1)
    source = (lane - word) & (LANES - 1)
    return source, source > lane


def by_plane(sums, word):
    picked = jnp.where(word < 3 * LANES, sums[:, 2 * LANES :], 0.0)
    picked = jnp.where(word < 2 * LANES, sums[:, LANES : 2 * LANES], picked)
    return jnp.where(word < LANES, sums[:, :LANES], picked)


def start_all(pairs, sems):
    copies = [
        pltpu.make_async_copy(source, target, sems.at[i])
        for i, (source, target) in enumerate(pairs)
    ]
    for copy in copies:
        copy.start()
    return copies


def cut_kernel(wave, *refs):
    tails, sems = refs[:-1], refs[-1]
    pairs = []
    first = 0
    for tail in tails:
        pairs.append((wave.at[pl.ds(first, tail.shape[0]), LANES:], tail))
        first += tail.shape[0]
    for copy in start_all(pairs, sems):
        copy.wait()


def response_kernel(wires_by_plane, *refs):
    make_responses(wires_by_plane, refs[0:3], refs[3:6], refs[6], refs[7], refs[8:11])


def fill_table(kernel_taps, wide_taps, table_out):
    r = lax.broadcasted_iota(jnp.int32, (LANES, LANES), 0)
    l = lax.broadcasted_iota(jnp.int32, (LANES, LANES), 1)
    wide_taps[...] = jnp.zeros_like(wide_taps)
    wide_taps[0:3, 0 : kernel_taps.shape[1]] = kernel_taps[...].astype(jnp.float32)
    for plane in range(3):
        rolled = lane_roll(wide_taps[plane : plane + 1, :], LANES)
        cols = slice(plane * LANES, (plane + 1) * LANES)
        table_out[:LANES, cols] = jnp.where(l < r, rolled, 0.0).astype(jnp.bfloat16)
        table_out[LANES:, cols] = jnp.where(l >= r, rolled, 0.0).astype(jnp.bfloat16)


def filter_window(wires_by_plane, side, front, tails, small, table, outs, words):
    high_out, low_out, code_out = outs
    slots, offset_rows, bad_rows = small
    one, two = wires_by_plane[0], wires_by_plane[0] + wires_by_plane[1]
    slot = slots[...]
    planes = (slot >= one).astype(jnp.int32) + (slot >= two).astype(jnp.int32)
    planes = jnp.where(bad_rows[...] == 0, planes, 3)
    words[...] = offset_rows[...] + LANES * planes
    groups = front.shape[0] // LANES
    for i in range(groups):
        row = jnp.broadcast_to(words[pl.ds(side[0] * groups + i, 1), :], (LANES, LANES))
        code_out[i * LANES : (i + 1) * LANES, :] = row.T

    first = 0
    for tail in tails:
        step = block_rows(tail.shape[0])
        for top in range(0, tail.shape[0], step):
            rows = slice(first + top, first + top + step)
            word = code_out[rows, :]
            source, wrapped = delays(word)
            early = take_lanes(front[rows, :].astype(jnp.float32), source)
            late = take_lanes(tail[top : top + step, :].astype(jnp.float32), source)
            low = jnp.where(wrapped, 0.0, early).astype(jnp.bfloat16)
            both = jnp.concatenate([early, jnp.where(wrapped, early, late)], 1)
            low_sum = jnp.dot(low, table[LANES:, :], preferred_element_type=jnp.float32)
            high_sum = jnp.dot(
                both.astype(jnp.bfloat16), table[...], preferred_element_type=jnp.float32
            )
            low_out[rows, :] = by_plane(low_sum, word)
            high_out[rows, :] = by_plane(high_sum, word).astype(jnp.bfloat16)
        first += tail.shape[0]


def window_kernel(wires_by_plane, count, side, first_tail, last_tail, wave, *refs):
    sources, refs = refs[:count], refs[count:]
    high_out, low_out, code_out, table_out = refs[:4]
    slot_outs, refs = refs[4:8], refs[2:]
    kept = refs[6 : 6 + count - 4]
    front, slots, offset_rows, bad_rows, kernel_taps, words, wide_taps, sems = refs[6 + count - 4 :]
    held = (slots, offset_rows, bad_rows, kernel_taps)
    copies = start_all(
        [*zip(sources[:4], held), (wave.at[:, :LANES], front), *zip(sources[4:], kept)], sems
    )
    for copy in copies[:5]:
        copy.wait()
    fill_table(kernel_taps, wide_taps, table_out)
    groups = front.shape[0] // LANES
    for i, out in enumerate(slot_outs):
        own = side[0] if i < 2 else 1 - side[0]
        skipped = slot_outs[0].shape[0] if i % 2 else 0
        out[...] = slots[pl.ds(own * groups + skipped, out.shape[0]), :]
    small = (slots, offset_rows, bad_rows)
    outs = (high_out, low_out, code_out)
    filter_window(wires_by_plane, side, front, (first_tail, last_tail), small, table_out, outs, words)
    for copy in copies[5:]:
        copy.wait()


def finish_early(halo, code, table, low_main, write):
    step = block_rows(halo.shape[0])

    def body(i, carry):
        rows = pl.ds(pl.multiple_of(i * step, step), step)
        word = code[rows, :]
        source, wrapped = delays(word)
        early = take_lanes(halo[rows, :].astype(jnp.float32), source)
        both = jnp.concatenate([early, jnp.where(wrapped, early, 0.0)], 1).astype(jnp.bfloat16)
        sums = jnp.dot(both, table[...], preferred_element_type=jnp.float32)
        write(rows, (low_main[rows, :] + by_plane(sums, word)).astype(jnp.bfloat16))
        return carry

    lax.fori_loop(0, halo.shape[0] // step, body, 0, unroll=True)


def other_kernel(first, side, halo, table, high, low_main, code, out):
    rows = pl.ds(first, out.shape[0])

    @pl.when(side[0] == 0)
    def _():
        out[...] = high[rows, :]

    @pl.when(side[0] != 0)
    def _():
        def write(here, value):
            out[here, :] = value

        finish_early(halo, code.at[rows], table, low_main.at[rows], write)


def finish_own(side, halo, table, high, low_main, code, wide):
    @pl.when(side[0] == 0)
    def _():
        def write(rows, value):
            wide[rows, :] = value.astype(jnp.float32)

        finish_early(halo, code, table, low_main, write)

    @pl.when(side[0] != 0)
    def _():
        wide[0 : high.shape[0], :] = high[...].astype(jnp.float32)


def place_rows(count, wide, slots, first, target):
    for k in range(count):
        slot = slots[(first + k) // LANES, (first + k) % LANES]
        target[pl.ds(slot, 1), :] = wide[k : k + 1, :]


def place_kernel(far, other, target, wide, slots, sem):
    copy = pltpu.make_async_copy(far, slots, sem.at[0])
    copy.start()
    wide[...] = other[...].astype(jnp.float32)
    copy.wait()
    place_rows(other.shape[0], wide, slots, 0, target)


def own_kernel(side, near, halo, table, high, low_main, code, before, target, wide, slots, sem):
    del before
    copy = pltpu.make_async_copy(near, slots, sem.at[0])
    copy.start()
    finish_own(side, halo, table, high.at[pl.ds(0, halo.shape[0])], low_main, code, wide)
    copy.wait()
    place_rows(halo.shape[0], wide, slots, 0, target)


def final_kernel(layout, first, side, near, far, other, halo, table, high, low_main, code, before, *refs):
    responses, out, ordered = refs[:3], refs[3], refs[4]
    wide, wide_other, mixed, near_slots, far_slots, sems = refs[5:]
    del before
    own = pl.ds(first, halo.shape[0])
    high, low_main, code = high.at[own], low_main.at[own], code.at[own]
    loads = [
        pltpu.make_async_copy(near, near_slots, sems.at[0]),
        pltpu.make_async_copy(far, far_slots, sems.at[1]),
    ]
    for load in loads:
        load.start()
    wide_other[...] = other[...].astype(jnp.float32)
    finish_own(side, halo, table, high, low_main, code, wide)
    for load in loads:
        load.wait()
    place_rows(other.shape[0], wide_other, far_slots, 0, ordered)
    place_rows(halo.shape[0], wide, near_slots, 0, ordered)
    copies = []
    for (start, wires), resp in zip(layout, responses):
        half = wires // 2
        base = padded(half)
        front = ordered[start : start + half, :]
        back = ordered[start + half : start + wires, :]
        total = (front + back).astype(jnp.bfloat16)
        change = (front - back).astype(jnp.bfloat16)
        sizes = [min(LANES, half - top) for top in range(0, half, LANES)]

        def rows_of(part):
            lefts = [base - block * LANES for block in range(len(sizes))]
            pieces = [
                resp[part * LANES : part * LANES + size, left : left + half]
                for size, left in zip(sizes, lefts)
            ]
            return jnp.concatenate(pieces, 0)

        even = jnp.dot(rows_of(0), total, preferred_element_type=jnp.float32)
        odd = jnp.dot(rows_of(1), change, preferred_element_type=jnp.float32)
        mixed[start : start + half, :] = even + odd
        mixed[start + half : start + wires, :] = even - odd
        span = pl.ds(start, wires)
        copies.append(pltpu.make_async_copy(mixed.at[span], out.at[span], sems.at[2 + len(copies)]))
        copies[-1].start()
    for copy in copies:
        copy.wait()


def deconvolve(
    waveforms,
    time_kernel,
    wire_slot,
    tick_offset,
    bad_channel,
    induction_real,
    induction_imaginary,
    induction_filter,
    collection_real,
    collection_imaginary,
    collection_filter,
):
    induction = induction_real.shape[1]
    collection = collection_real.shape[0]
    wires_by_plane = (induction, induction, collection)
    taps = time_kernel.shape[1]
    rows, ticks = waveforms.shape
    channels = wire_slot.shape[0]
    assert ticks == 2 * LANES and taps + OFFSET_RANGE == LANES
    assert channels == 2 * rows and channels == 2 * induction + collection
    parts = (rows - LAST_ROWS, LAST_ROWS)

    vm = pl.BlockSpec(memory_space=VMEM)
    sm = pl.BlockSpec(memory_space=SMEM)
    hbm = pl.BlockSpec(memory_space=pltpu.HBM)
    keep = functools.partial(pltpu.with_memory_space_constraint, memory_space=pltpu.HBM)
    shape = jax.ShapeDtypeStruct
    side = lax.axis_index("apa")
    side_word = side.reshape(1).astype(jnp.int32)

    def call(kernel, outs, operands, specs, scratch, flops, **more):
        return pl.pallas_call(
            kernel,
            out_shape=outs,
            in_specs=specs,
            out_specs=more.pop("out_specs", [vm] * len(outs)),
            scratch_shapes=scratch,
            compiler_params=pltpu.CompilerParams(vmem_limit_bytes=KERNEL_VMEM),
            cost_estimate=pl.CostEstimate(flops=flops, bytes_accessed=10**6, transcendentals=0),
            **more,
        )(*operands)

    def by_lanes(vector):
        return vector.reshape(channels // LANES, LANES)

    def like(array):
        return shape(array.shape, array.dtype)

    small = [
        by_lanes(wire_slot),
        by_lanes(tick_offset),
        by_lanes(bad_channel),
        time_kernel,
        induction_real,
        induction_imaginary,
        induction_filter,
        collection_real[None],
        collection_imaginary[None],
        collection_filter[None],
    ]
    first_tail, last_tail = call(
        cut_kernel,
        [shape((count, LANES), waveforms.dtype) for count in parts],
        [keep(waveforms)],
        [hbm],
        [pltpu.SemaphoreType.DMA((2,))],
        10**5,
    )

    groups, ring = lax.axis_size("grp"), lax.axis_size("tm")
    axes = ("grp", "tm", "apa")

    def onward(core):
        pairs = []
        for g in range(groups):
            for t in range(ring):
                here = 2 * (g * ring + t)
                pairs.append((here + core, 2 * (g * ring + (t + 1) % ring) + core))
                pairs.append((here + 1 - core, 2 * ((g + 1) % groups * ring + t) + 1 - core))
        return pairs

    halos = {}
    for name, part in (("first", first_tail), ("last", last_tail)):
        for core, whose in ((1, "other"), (0, "own")):
            halos[whose, name] = lax.ppermute(part, axes, onward(core))

    constants = [jnp.asarray(t) for t in wire_tables(wires_by_plane)]
    sources = [*small, *constants]
    slot_shapes = [shape((count // LANES, LANES), jnp.int32) for count in parts] * 2
    window = call(
        functools.partial(window_kernel, wires_by_plane, len(sources)),
        [
            shape((rows, LANES), jnp.bfloat16),
            shape((rows, LANES), jnp.float32),
            shape((rows, LANES), jnp.int32),
            shape((2 * LANES, 3 * LANES), jnp.bfloat16),
            *slot_shapes,
        ]
        + [like(x) for x in sources[4:]],
        [side_word, first_tail, last_tail, *map(keep, [waveforms, *sources])],
        [sm, vm, vm] + [hbm] * (1 + len(sources)),
        [pltpu.VMEM((rows, LANES), jnp.bfloat16)]
        + [pltpu.VMEM(x.shape, x.dtype) for x in small[:4]]
        + [
            pltpu.VMEM((channels // LANES, LANES), jnp.int32),
            pltpu.VMEM((8, LANES), jnp.float32),
            pltpu.SemaphoreType.DMA((1 + len(sources),)),
        ],
        10**9,
    )
    own_part = window[:3]
    table, near_first, near_last, far_first, far_last = window[3:8]
    responses = call(
        functools.partial(response_kernel, wires_by_plane),
        [shape((2 * LANES, 2 * padded(w // 2)), jnp.bfloat16) for w in wires_by_plane],
        list(window[8:]),
        [vm] * 8,
        [],
        10**9,
    )

    received = []
    for name, first in (("first", 0), ("last", parts[0])):
        halo = halos["other", name]
        (other,) = call(
            functools.partial(other_kernel, first),
            [shape(halo.shape, halo.dtype)],
            [side_word, halo, table, *own_part],
            [sm] + [vm] * 5,
            [],
            10**8,
        )
        received.append(lax.ppermute(other, "apa", [(0, 1), (1, 0)]))
    placing = [
        pltpu.VMEM((parts[0], LANES), jnp.float32),
        pltpu.SMEM(slot_shapes[0].shape, jnp.int32),
        pltpu.SemaphoreType.DMA((1,)),
    ]
    (placed,) = call(
        place_kernel,
        [shape((channels, LANES), jnp.float32)],
        [far_first, received[0]],
        [vm] * 2,
        placing,
        10**8,
    )
    (placed,) = call(
        own_kernel,
        [shape((channels, LANES), jnp.float32)],
        [side_word, near_first, halos["own", "first"], table, *own_part, placed],
        [sm] + [vm] * 7,
        placing,
        10**8,
        input_output_aliases={7: 0},
    )

    layout = []
    start = 0
    for wires in wires_by_plane:
        layout.append((start, wires))
        start += wires
    return call(
        functools.partial(final_kernel, layout, parts[0]),
        [shape((channels, LANES), jnp.float32)] * 2,
        [side_word, near_last, far_last, received[1], halos["own", "last"], table, *own_part, placed, *responses],
        [sm] + [vm] * 12,
        [
            pltpu.VMEM((parts[1], LANES), jnp.float32),
            pltpu.VMEM((parts[1], LANES), jnp.float32),
            pltpu.VMEM((channels, LANES), jnp.float32),
            pltpu.SMEM(slot_shapes[1].shape, jnp.int32),
            pltpu.SMEM(slot_shapes[1].shape, jnp.int32),
            pltpu.SemaphoreType.DMA((5,)),
        ],
        10**9,
        out_specs=[pl.BlockSpec(memory_space=pl.ANY), vm],
        input_output_aliases={9: 1},
    )[0]


def solution(mesh):
    placed = (P(("grp", "apa"), "tm"), P(), P("grp"), P("grp"), P("grp")) + (P(),) * 6
    return jax.shard_map(
        deconvolve, mesh=mesh, in_specs=placed, out_specs=P("grp", ("tm", "apa")), check_vma=False
    )
```

```python
import functools
import math

import jax
import jax.numpy as jnp
import numpy as np
from jax import lax
from jax.experimental import pallas as pl
from jax.experimental.pallas import tpu as pltpu
from jax.sharding import PartitionSpec as P


OFFSET_RANGE = 64
LANES = 128
VMEM = pltpu.VMEM
SMEM = pltpu.SMEM
KERNEL_VMEM = 16 * 2**20
BLOCKS = (448, 384, 320, 256, 128)
LAST_ROWS = 384


def block_rows(count):
    return next(size for size in BLOCKS if count % size == 0)


def padded(count):
    return -(-count // LANES) * LANES


def frequency_classes(wires):
    return [(0, 4, wires // 4), (2, 4, wires // 4), (1, 2, wires // 2)]


def wire_tables(wires_by_plane):
    widest = max(wires_by_plane)
    coarse_rows, fine_rows = [], []
    for wires in wires_by_plane[1:]:
        m = np.arange(wires, dtype=np.int64)
        turn = 2.0 * math.pi / wires
        parts = []
        for first, step, length in frequency_classes(wires):
            base = padded(length)
            k = np.arange(2 * base // LANES, dtype=np.int64)[:, None] * LANES - base
            angle = k * m[None, :] % wires * turn
            parts.append((angle, (m % step == first)[None, :]))
        for function in (np.cos, np.sin):
            for angle, chosen in parts:
                full = np.zeros((angle.shape[0], widest), np.float32)
                full[:, :wires] = function(angle) * chosen
                coarse_rows.append(full)
        fine = m[:, None] * np.arange(LANES, dtype=np.int64)[None, :] % wires * turn
        fine_rows.append(np.concatenate([np.cos(fine), np.sin(fine)], 1).astype(np.float32))
    fine = np.concatenate(fine_rows, 0)
    high = fine.astype(jnp.bfloat16)
    low = (fine - high.astype(np.float32)).astype(jnp.bfloat16)
    return np.concatenate(coarse_rows, 0), np.concatenate([high, low], 1)


def take_lanes(rows, lanes):
    return lax.gather(
        rows,
        lanes[..., None],
        lax.GatherDimensionNumbers(
            offset_dims=(),
            collapsed_slice_dims=(1,),
            start_index_map=(1,),
            operand_batching_dims=(0,),
            start_indices_batching_dims=(0,),
        ),
        slice_sizes=(1, 1),
        mode=lax.GatherScatterMode.PROMISE_IN_BOUNDS,
    )


def lane_roll(row, rows):
    r = lax.broadcasted_iota(jnp.int32, (rows, LANES), 0)
    l = lax.broadcasted_iota(jnp.int32, (rows, LANES), 1)
    return take_lanes(jnp.broadcast_to(row, (rows, LANES)), (l - r) & (LANES - 1))


def split_dot(left, high, low):
    upper = left.astype(jnp.bfloat16)
    lower = (left - upper.astype(jnp.float32)).astype(jnp.bfloat16)
    rows = left.shape[0]
    both = jnp.dot(
        jnp.concatenate([upper, lower], 0), high, preferred_element_type=jnp.float32
    )
    return both[:rows] + both[rows:] + jnp.dot(upper, low, preferred_element_type=jnp.float32)


def make_responses(wires_by_plane, induction, collection, coarse, fine, outs):
    r = lax.broadcasted_iota(jnp.int32, (LANES, LANES), 0)
    l = lax.broadcasted_iota(jnp.int32, (LANES, LANES), 1)
    for plane, wires in enumerate(wires_by_plane):
        out = outs[plane]
        spans = [2 * padded(length) // LANES for _, _, length in frequency_classes(wires)]
        total = sum(spans)
        first = 0 if plane < 2 else coarse.shape[0] - 2 * total
        ca = coarse[first : first + total, :wires]
        sa = coarse[first + total : first + 2 * total, :wires]
        first = 0 if plane < 2 else wires_by_plane[0]
        rows = slice(first, first + wires)
        if plane < 2:
            real, imag, gain = (ref[plane : plane + 1, :] for ref in induction)
        else:
            real, imag, gain = (ref[...] for ref in collection)
        scale = gain / (real * real + imag * imag) * (1.0 / wires)
        ratio_re = real * scale
        ratio_im = -imag * scale
        u = ca * ratio_re + sa * ratio_im
        v = ca * ratio_im - sa * ratio_re
        taps = split_dot(u, fine[rows, :LANES], fine[rows, 2 * LANES : 3 * LANES])
        taps = taps + split_dot(v, fine[rows, LANES : 2 * LANES], fine[rows, 3 * LANES :])
        row = 0
        for part, count in enumerate(spans):
            top = slice(part * LANES, (part + 1) * LANES)
            previous = None
            for span in range(count):
                here = lane_roll(taps[row : row + 1, :], LANES)
                before = here if previous is None else previous
                out[top, span * LANES : (span + 1) * LANES] = jnp.where(l >= r, here, before).astype(
                    jnp.bfloat16
                )
                previous = here
                row += 1


def delays(word):
    lane = lax.broadcasted_iota(jnp.int32, word.shape, 1)
    source = (lane - word) & (LANES - 1)
    return source, source > lane


def by_plane(sums, word):
    picked = jnp.where(word < 3 * LANES, sums[:, 2 * LANES :], 0.0)
    picked = jnp.where(word < 2 * LANES, sums[:, LANES : 2 * LANES], picked)
    return jnp.where(word < LANES, sums[:, :LANES], picked)


def start_all(pairs, sems):
    copies = [
        pltpu.make_async_copy(source, target, sems.at[i])
        for i, (source, target) in enumerate(pairs)
    ]
    for copy in copies:
        copy.start()
    return copies


def cut_kernel(wave, *refs):
    tails, sems = refs[:-1], refs[-1]
    pairs = []
    first = 0
    for tail in tails:
        pairs.append((wave.at[pl.ds(first, tail.shape[0]), LANES:], tail))
        first += tail.shape[0]
    for copy in start_all(pairs, sems):
        copy.wait()


def response_kernel(wires_by_plane, *refs):
    make_responses(wires_by_plane, refs[0:3], refs[3:6], refs[6], refs[7], refs[8:11])


def fill_table(kernel_taps, wide_taps, table_out):
    r = lax.broadcasted_iota(jnp.int32, (LANES, LANES), 0)
    l = lax.broadcasted_iota(jnp.int32, (LANES, LANES), 1)
    wide_taps[...] = jnp.zeros_like(wide_taps)
    wide_taps[0:3, 0 : kernel_taps.shape[1]] = kernel_taps[...].astype(jnp.float32)
    for plane in range(3):
        rolled = lane_roll(wide_taps[plane : plane + 1, :], LANES)
        cols = slice(plane * LANES, (plane + 1) * LANES)
        table_out[:LANES, cols] = jnp.where(l < r, rolled, 0.0).astype(jnp.bfloat16)
        table_out[LANES:, cols] = jnp.where(l >= r, rolled, 0.0).astype(jnp.bfloat16)


def filter_window(wires_by_plane, side, front, tails, small, table, outs, words):
    high_out, low_out, code_out = outs
    slots, offset_rows, bad_rows = small
    one, two = wires_by_plane[0], wires_by_plane[0] + wires_by_plane[1]
    slot = slots[...]
    planes = (slot >= one).astype(jnp.int32) + (slot >= two).astype(jnp.int32)
    planes = jnp.where(bad_rows[...] == 0, planes, 3)
    words[...] = offset_rows[...] + LANES * planes
    groups = front.shape[0] // LANES
    for i in range(groups):
        row = jnp.broadcast_to(words[pl.ds(side[0] * groups + i, 1), :], (LANES, LANES))
        code_out[i * LANES : (i + 1) * LANES, :] = row.T

    first = 0
    for tail in tails:
        step = block_rows(tail.shape[0])
        for top in range(0, tail.shape[0], step):
            rows = slice(first + top, first + top + step)
            word = code_out[rows, :]
            source, wrapped = delays(word)
            early = take_lanes(front[rows, :].astype(jnp.float32), source)
            late = take_lanes(tail[top : top + step, :].astype(jnp.float32), source)
            low = jnp.where(wrapped, 0.0, early).astype(jnp.bfloat16)
            both = jnp.concatenate([early, jnp.where(wrapped, early, late)], 1)
            low_sum = jnp.dot(low, table[LANES:, :], preferred_element_type=jnp.float32)
            high_sum = jnp.dot(
                both.astype(jnp.bfloat16), table[...], preferred_element_type=jnp.float32
            )
            low_out[rows, :] = by_plane(low_sum, word)
            high_out[rows, :] = by_plane(high_sum, word).astype(jnp.bfloat16)
        first += tail.shape[0]


def window_kernel(wires_by_plane, count, side, first_tail, last_tail, wave, *refs):
    sources, refs = refs[:count], refs[count:]
    high_out, low_out, code_out, table_out = refs[:4]
    slot_outs, refs = refs[4:8], refs[2:]
    kept = refs[6 : 6 + count - 4]
    front, slots, offset_rows, bad_rows, kernel_taps, words, wide_taps, sems = refs[6 + count - 4 :]
    held = (slots, offset_rows, bad_rows, kernel_taps)
    copies = start_all(
        [*zip(sources[:4], held), (wave.at[:, :LANES], front), *zip(sources[4:], kept)], sems
    )
    for copy in copies[:5]:
        copy.wait()
    fill_table(kernel_taps, wide_taps, table_out)
    groups = front.shape[0] // LANES
    for i, out in enumerate(slot_outs):
        own = side[0] if i < 2 else 1 - side[0]
        skipped = slot_outs[0].shape[0] if i % 2 else 0
        out[...] = slots[pl.ds(own * groups + skipped, out.shape[0]), :]
    small = (slots, offset_rows, bad_rows)
    outs = (high_out, low_out, code_out)
    filter_window(wires_by_plane, side, front, (first_tail, last_tail), small, table_out, outs, words)
    for copy in copies[5:]:
        copy.wait()


def finish_early(halo, code, table, low_main, write):
    step = block_rows(halo.shape[0])

    def body(i, carry):
        rows = pl.ds(pl.multiple_of(i * step, step), step)
        word = code[rows, :]
        source, wrapped = delays(word)
        early = take_lanes(halo[rows, :].astype(jnp.float32), source)
        both = jnp.concatenate([early, jnp.where(wrapped, early, 0.0)], 1).astype(jnp.bfloat16)
        sums = jnp.dot(both, table[...], preferred_element_type=jnp.float32)
        write(rows, (low_main[rows, :] + by_plane(sums, word)).astype(jnp.bfloat16))
        return carry

    lax.fori_loop(0, halo.shape[0] // step, body, 0, unroll=True)


def other_kernel(first, side, halo, table, high, low_main, code, out):
    rows = pl.ds(first, out.shape[0])

    @pl.when(side[0] == 0)
    def _():
        out[...] = high[rows, :]

    @pl.when(side[0] != 0)
    def _():
        def write(here, value):
            out[here, :] = value

        finish_early(halo, code.at[rows], table, low_main.at[rows], write)


def finish_own(side, halo, table, high, low_main, code, wide):
    @pl.when(side[0] == 0)
    def _():
        def write(rows, value):
            wide[rows, :] = value.astype(jnp.float32)

        finish_early(halo, code, table, low_main, write)

    @pl.when(side[0] != 0)
    def _():
        wide[0 : high.shape[0], :] = high[...].astype(jnp.float32)


def place_rows(count, wide, slots, first, target):
    for k in range(count):
        slot = slots[(first + k) // LANES, (first + k) % LANES]
        target[pl.ds(slot, 1), :] = wide[k : k + 1, :]


def place_kernel(far, other, target, wide, slots, sem):
    copy = pltpu.make_async_copy(far, slots, sem.at[0])
    copy.start()
    wide[...] = other[...].astype(jnp.float32)
    copy.wait()
    place_rows(other.shape[0], wide, slots, 0, target)


def own_kernel(side, near, halo, table, high, low_main, code, before, target, wide, slots, sem):
    del before
    copy = pltpu.make_async_copy(near, slots, sem.at[0])
    copy.start()
    finish_own(side, halo, table, high.at[pl.ds(0, halo.shape[0])], low_main, code, wide)
    copy.wait()
    place_rows(halo.shape[0], wide, slots, 0, target)


def final_kernel(layout, first, side, near, far, other, halo, table, high, low_main, code, before, *refs):
    responses, out, ordered = refs[:3], refs[3], refs[4]
    wide, wide_other, mixed, near_slots, far_slots, sems = refs[5:]
    del before
    own = pl.ds(first, halo.shape[0])
    high, low_main, code = high.at[own], low_main.at[own], code.at[own]
    loads = [
        pltpu.make_async_copy(near, near_slots, sems.at[0]),
        pltpu.make_async_copy(far, far_slots, sems.at[1]),
    ]
    for load in loads:
        load.start()
    wide_other[...] = other[...].astype(jnp.float32)
    finish_own(side, halo, table, high, low_main, code, wide)
    for load in loads:
        load.wait()
    place_rows(other.shape[0], wide_other, far_slots, 0, ordered)
    place_rows(halo.shape[0], wide, near_slots, 0, ordered)
    copies = []

    def product(resp, part, length, data):
        pieces = []
        for top in range(0, length, LANES):
            rows = slice(part * LANES, part * LANES + min(LANES, length - top))
            left = padded(length) - top
            pieces.append(resp[rows, left : left + length])
        return jnp.dot(jnp.concatenate(pieces, 0), data, preferred_element_type=jnp.float32)

    for (start, wires), resp in zip(layout, responses):
        half, quarter = wires // 2, wires // 4
        front = ordered[start : start + half, :]
        back = ordered[start + half : start + wires, :]
        total = front + back
        change = (front - back).astype(jnp.bfloat16)
        plus = product(resp, 0, quarter, (total[:quarter] + total[quarter:]).astype(jnp.bfloat16))
        minus = product(resp, 1, quarter, (total[:quarter] - total[quarter:]).astype(jnp.bfloat16))
        even = jnp.concatenate([plus + minus, plus - minus], 0)
        odd = product(resp, 2, half, change)
        mixed[start : start + half, :] = even + odd
        mixed[start + half : start + wires, :] = even - odd
        span = pl.ds(start, wires)
        copies.append(pltpu.make_async_copy(mixed.at[span], out.at[span], sems.at[2 + len(copies)]))
        copies[-1].start()
    for copy in copies:
        copy.wait()


def deconvolve(
    waveforms,
    time_kernel,
    wire_slot,
    tick_offset,
    bad_channel,
    induction_real,
    induction_imaginary,
    induction_filter,
    collection_real,
    collection_imaginary,
    collection_filter,
):
    induction = induction_real.shape[1]
    collection = collection_real.shape[0]
    wires_by_plane = (induction, induction, collection)
    taps = time_kernel.shape[1]
    rows, ticks = waveforms.shape
    channels = wire_slot.shape[0]
    assert ticks == 2 * LANES and taps + OFFSET_RANGE == LANES
    assert channels == 2 * rows and channels == 2 * induction + collection
    assert induction % 4 == 0 and collection % 4 == 0
    parts = (rows - LAST_ROWS, LAST_ROWS)

    vm = pl.BlockSpec(memory_space=VMEM)
    sm = pl.BlockSpec(memory_space=SMEM)
    hbm = pl.BlockSpec(memory_space=pltpu.HBM)
    keep = functools.partial(pltpu.with_memory_space_constraint, memory_space=pltpu.HBM)
    shape = jax.ShapeDtypeStruct
    side = lax.axis_index("apa")
    side_word = side.reshape(1).astype(jnp.int32)

    def call(kernel, outs, operands, specs, scratch, flops, **more):
        return pl.pallas_call(
            kernel,
            out_shape=outs,
            in_specs=specs,
            out_specs=more.pop("out_specs", [vm] * len(outs)),
            scratch_shapes=scratch,
            compiler_params=pltpu.CompilerParams(vmem_limit_bytes=KERNEL_VMEM),
            cost_estimate=pl.CostEstimate(flops=flops, bytes_accessed=10**6, transcendentals=0),
            **more,
        )(*operands)

    def by_lanes(vector):
        return vector.reshape(channels // LANES, LANES)

    def like(array):
        return shape(array.shape, array.dtype)

    small = [
        by_lanes(wire_slot),
        by_lanes(tick_offset),
        by_lanes(bad_channel),
        time_kernel,
        induction_real,
        induction_imaginary,
        induction_filter,
        collection_real[None],
        collection_imaginary[None],
        collection_filter[None],
    ]
    first_tail, last_tail = call(
        cut_kernel,
        [shape((count, LANES), waveforms.dtype) for count in parts],
        [keep(waveforms)],
        [hbm],
        [pltpu.SemaphoreType.DMA((2,))],
        10**5,
    )

    groups, ring = lax.axis_size("grp"), lax.axis_size("tm")
    axes = ("grp", "tm", "apa")

    def onward(core):
        pairs = []
        for g in range(groups):
            for t in range(ring):
                here = 2 * (g * ring + t)
                pairs.append((here + core, 2 * (g * ring + (t + 1) % ring) + core))
                pairs.append((here + 1 - core, 2 * ((g + 1) % groups * ring + t) + 1 - core))
        return pairs

    halos = {}
    for name, part in (("first", first_tail), ("last", last_tail)):
        for core, whose in ((1, "other"), (0, "own")):
            halos[whose, name] = lax.ppermute(part, axes, onward(core))

    constants = [jnp.asarray(t) for t in wire_tables(wires_by_plane)]
    sources = [*small, *constants]
    slot_shapes = [shape((count // LANES, LANES), jnp.int32) for count in parts] * 2
    window = call(
        functools.partial(window_kernel, wires_by_plane, len(sources)),
        [
            shape((rows, LANES), jnp.bfloat16),
            shape((rows, LANES), jnp.float32),
            shape((rows, LANES), jnp.int32),
            shape((2 * LANES, 3 * LANES), jnp.bfloat16),
            *slot_shapes,
        ]
        + [like(x) for x in sources[4:]],
        [side_word, first_tail, last_tail, *map(keep, [waveforms, *sources])],
        [sm, vm, vm] + [hbm] * (1 + len(sources)),
        [pltpu.VMEM((rows, LANES), jnp.bfloat16)]
        + [pltpu.VMEM(x.shape, x.dtype) for x in small[:4]]
        + [
            pltpu.VMEM((channels // LANES, LANES), jnp.int32),
            pltpu.VMEM((8, LANES), jnp.float32),
            pltpu.SemaphoreType.DMA((1 + len(sources),)),
        ],
        10**9,
    )
    own_part = window[:3]
    table, near_first, near_last, far_first, far_last = window[3:8]
    responses = call(
        functools.partial(response_kernel, wires_by_plane),
        [shape((3 * LANES, 2 * padded(w // 2)), jnp.bfloat16) for w in wires_by_plane],
        list(window[8:]),
        [vm] * 8,
        [],
        10**9,
    )

    received = []
    for name, first in (("first", 0), ("last", parts[0])):
        halo = halos["other", name]
        (other,) = call(
            functools.partial(other_kernel, first),
            [shape(halo.shape, halo.dtype)],
            [side_word, halo, table, *own_part],
            [sm] + [vm] * 5,
            [],
            10**8,
        )
        received.append(lax.ppermute(other, "apa", [(0, 1), (1, 0)]))
    placing = [
        pltpu.VMEM((parts[0], LANES), jnp.float32),
        pltpu.SMEM(slot_shapes[0].shape, jnp.int32),
        pltpu.SemaphoreType.DMA((1,)),
    ]
    (placed,) = call(
        place_kernel,
        [shape((channels, LANES), jnp.float32)],
        [far_first, received[0]],
        [vm] * 2,
        placing,
        10**8,
    )
    (placed,) = call(
        own_kernel,
        [shape((channels, LANES), jnp.float32)],
        [side_word, near_first, halos["own", "first"], table, *own_part, placed],
        [sm] + [vm] * 7,
        placing,
        10**8,
        input_output_aliases={7: 0},
    )

    layout = []
    start = 0
    for wires in wires_by_plane:
        layout.append((start, wires))
        start += wires
    return call(
        functools.partial(final_kernel, layout, parts[0]),
        [shape((channels, LANES), jnp.float32)] * 2,
        [side_word, near_last, far_last, received[1], halos["own", "last"], table, *own_part, placed, *responses],
        [sm] + [vm] * 12,
        [
            pltpu.VMEM((parts[1], LANES), jnp.float32),
            pltpu.VMEM((parts[1], LANES), jnp.float32),
            pltpu.VMEM((channels, LANES), jnp.float32),
            pltpu.SMEM(slot_shapes[1].shape, jnp.int32),
            pltpu.SMEM(slot_shapes[1].shape, jnp.int32),
            pltpu.SemaphoreType.DMA((5,)),
        ],
        10**9,
        out_specs=[pl.BlockSpec(memory_space=pl.ANY), vm],
        input_output_aliases={9: 1},
    )[0]


def solution(mesh):
    placed = (P(("grp", "apa"), "tm"), P(), P("grp"), P("grp"), P("grp")) + (P(),) * 6
    return jax.shard_map(
        deconvolve, mesh=mesh, in_specs=placed, out_specs=P("grp", ("tm", "apa")), check_vma=False
    )
```
